128 devices in a mesh: dp: 16 (over x, z), blk: 8 (over y, core).
Axes of the slice: x: 4, y: 4, z: 4, core: 2. Of those that a mesh axis runs over, the one named last changes fastest.
Arguments:
- entity_table: float32 [262144, 400], P(('dp', 'blk')), may hold values from -1.8 to 1.8
- adagrad_sum: float32 [262144], P(('dp', 'blk')), may hold values from 0.0001 to 0.001
- relations: float32 [7424, 400], replicated, may hold values from -1.8 to 1.8
- owner_map: int32 [262144], replicated, may hold values from 0 to 262143, as said below
- head_ids: int32 [16384], P(('dp', 'blk')), may hold values from 0 to 262143, as said below
- rel_ids: int32 [16384], P(('dp', 'blk')), may hold values from 0 to 7423
- tail_ids: int32 [16384], P(('dp', 'blk')), may hold values from 0 to 262143, as said below
- neg_ids: int32 [65536], P(('dp', 'blk')), may hold values from 0 to 262143, as said below
Outputs:
- new_table: float32 [262144, 400], P(('dp', 'blk'))
- new_sum: float32 [262144], P(('dp', 'blk'))
The draws below stay inside these ranges and needn't reach their ends.
Inputs may be any that keep to these rules, and one draw needn't show every extreme that they name: `owner_map`: A permutation: every storage position appears once. The owner of position p is device p // 2048. `head_ids`: among the 128 heads, 128 tails and 512 negatives of one device taken together, at most 12 are stored on any one owner; in every draw 16 owners receive exactly 12 from every device. `tail_ids`: counted together with the heads and negatives of the same device, as stated for head_ids. `neg_ids`: counted together with the heads and tails of the same device, as stated for head_ids.
All inputs are finite; a program needn't handle non-finite values.
Results may differ from the reference program's by a relative error of at most 0.00005.
Values sent between devices are 32-bit elements; how exact they have to be, the bound alone decides.
A program may use at most 128 MiB of HBM per device.

```python
import math
import jax
import jax.numpy as jnp
from jax import lax

DIM = 400
NREL = 7424
NEG = 512
ROWS_DEV = 2048
EDGES_DEV = 128
ENTITIES = 262144
EDGES = 16384
CAP = 12
NHOT = 16
N_DP = 16
N_BLK = 8


def draw_owner_map(key, part):
    return jax.random.permutation(jax.random.fold_in(key, 11), ENTITIES).astype(jnp.int32)


def request_layout(key):
    owner_total = ENTITIES // ROWS_DEV
    slot_total = owner_total * CAP
    request_total = 2 * EDGES_DEV + NEG
    placement = draw_owner_map(key, 0)
    inverse = jnp.argsort(placement).astype(jnp.int32)
    hot_owner = jax.random.permutation(jax.random.fold_in(key, 12), owner_total)[:NHOT]
    hot_flag = jnp.zeros((owner_total,), jnp.int32).at[hot_owner].set(1)
    slot_index = jnp.arange(slot_total, dtype=jnp.int32)
    slot_owner = slot_index // CAP
    device_keys = jax.random.split(jax.random.fold_in(key, 13), owner_total)

    def per_device(dev_key):
        jitter = jax.random.randint(jax.random.fold_in(dev_key, 1), (slot_total,), 0, 65536)
        ranking = (jitter + 131072 * hot_flag[slot_owner]) * slot_total + slot_index
        chosen = lax.top_k(ranking, request_total)[1].astype(jnp.int32)
        owner_of = chosen // CAP
        local_row = jax.random.randint(jax.random.fold_in(dev_key, 2), (request_total,), 0, ROWS_DEV)
        positions = owner_of * ROWS_DEV + local_row
        shuffle = jax.random.permutation(jax.random.fold_in(dev_key, 3), request_total)
        return inverse[positions[shuffle]]
    return jax.vmap(per_device)(device_keys).astype(jnp.int32)


def draw_head_ids(key, part):
    return request_layout(key)[:, :EDGES_DEV].reshape(-1)


def draw_tail_ids(key, part):
    return request_layout(key)[:, EDGES_DEV:2 * EDGES_DEV].reshape(-1)


def draw_neg_ids(key, part):
    return request_layout(key)[:, 2 * EDGES_DEV:].reshape(-1)


def set_ends(array, key, least, top_value):
    longest = array.shape.index(max(array.shape))
    spots = []
    for shift in (0, 1):
        where = [jax.random.randint(jax.random.fold_in(key, axis), (), 0, length) for axis, length in enumerate(array.shape)]
        where[longest] = (where[longest] + shift) % array.shape[longest]
        spots.append(tuple(where))
    return array.at[spots[0]].set(least).at[spots[1]].set(top_value)


def level_of(key, shape, pieces, least, top_value):
    level = 1.0
    for axis_at, blocks in pieces:
        heights = jax.random.uniform(jax.random.fold_in(jax.random.fold_in(key, 6), axis_at), (blocks,), jnp.float32, least / len(pieces), top_value / len(pieces))
        level = level * jnp.repeat(jnp.exp(heights), shape[axis_at] // blocks).reshape((-1,) + (1,) * (len(shape) - 1 - axis_at))
    return level


def bell_draw(own_key, shape, scale, reach, cuts=(), held_as=jnp.bfloat16):
    result = jax.random.normal(own_key, shape, jnp.float32) * scale
    if len(cuts) > 0:
        result = level_of(own_key, shape, cuts, -0.22, 0.18) * result
    return jnp.clip(result, min=-reach, max=reach).astype(held_as)


def setup_inputs(seed: int = 0) -> dict:
    streams_of = jax.random.split(jax.random.key(seed), 9)
    entity_table = bell_draw(streams_of[0], (ENTITIES, DIM), 0.3, 1.8, ((0, 128),), jnp.float32)
    adagrad_sum = jnp.clip(jnp.exp(math.log(0.001) - 2.3025852 * jax.random.uniform(streams_of[1], (ENTITIES,), jnp.float32) ** level_of(streams_of[1], (ENTITIES,), ((0, 128),), -0.2, 0.2)), 0.0001, 0.001)
    relations = bell_draw(streams_of[2], (NREL, DIM), 0.3, 1.8, (), jnp.float32)
    owner_map = draw_owner_map(jax.random.fold_in(streams_of[8], 71), 0)
    head_ids = draw_head_ids(jax.random.fold_in(streams_of[8], 71), 0)
    rel_ids = set_ends(jax.random.randint(streams_of[5], (EDGES,), 0, NREL), jax.random.fold_in(streams_of[5], 1), 0, NREL - 1).astype(jnp.int32)
    tail_ids = draw_tail_ids(jax.random.fold_in(streams_of[8], 71), 0)
    neg_ids = draw_neg_ids(jax.random.fold_in(streams_of[8], 71), 0)
    return dict(entity_table=entity_table, adagrad_sum=adagrad_sum, relations=relations, owner_map=owner_map, head_ids=head_ids, rel_ids=rel_ids, tail_ids=tail_ids, neg_ids=neg_ids)


MARGIN = 10.0
EPSILON = 1e-05
LEARNING_RATE = 0.1

def negative_terms(queries, neg_block, weight):
    query_sq = lax.optimization_barrier(jnp.sum(queries * queries, axis=1))
    block_sq = lax.optimization_barrier(jnp.sum(neg_block * neg_block, axis=1))
    inner_prod = jnp.dot(queries, neg_block.T, precision=lax.Precision.HIGHEST, preferred_element_type=jnp.float32)
    distance = jnp.sqrt(query_sq[:, None] + block_sq[None, :] - 2.0 * inner_prod + EPSILON)
    coefficient = -jax.nn.sigmoid(MARGIN - distance) / (weight * distance)
    grad_query = queries * lax.optimization_barrier(jnp.sum(coefficient, axis=1))[:, None] - jnp.dot(coefficient, neg_block, precision=lax.Precision.HIGHEST, preferred_element_type=jnp.float32)
    grad_block = neg_block * lax.optimization_barrier(jnp.sum(coefficient, axis=0))[:, None] - jnp.dot(coefficient.T, queries, precision=lax.Precision.HIGHEST, preferred_element_type=jnp.float32)
    return (grad_query, grad_block)

def reference(entity_table, adagrad_sum, relations, owner_map, head_ids, rel_ids, tail_ids, neg_ids):
    head_pos = owner_map[head_ids]
    tail_pos = owner_map[tail_ids]
    neg_pos = owner_map[neg_ids]
    queries = entity_table[head_pos] + relations[rel_ids]
    residue = queries - entity_table[tail_pos]
    pos_dist = jnp.sqrt(lax.optimization_barrier(jnp.sum(residue * residue, axis=1)) + EPSILON)
    grad_pos = (jax.nn.sigmoid(pos_dist - MARGIN) / pos_dist)[:, None] * residue
    weight = float(N_BLK * NEG)
    grouped_queries = queries.reshape(N_DP, N_BLK * EDGES_DEV, DIM)
    grouped_negs = entity_table[neg_pos].reshape(N_DP, N_BLK * NEG, DIM)

    def per_group(paired):
        return negative_terms(paired[0], paired[1], weight)
    grad_neg, block_grad = lax.map(per_group, (grouped_queries, grouped_negs))
    summed = jnp.zeros_like(entity_table)
    summed = summed.at[head_pos].add(grad_pos + grad_neg.reshape(-1, DIM))
    summed = summed.at[tail_pos].add(-grad_pos)
    summed = summed.at[neg_pos].add(block_grad.reshape(-1, DIM))
    new_sum = adagrad_sum + lax.optimization_barrier(jnp.mean(summed * summed, axis=1))
    new_table = entity_table - LEARNING_RATE * summed / jnp.sqrt(new_sum)[:, None]
    return (new_table, new_sum)
```

```python
import jax
import jax.numpy as jnp
from jax import lax
from jax.sharding import PartitionSpec as P

MARGIN = 10.0
EPSILON = 1e-05
LEARNING_RATE = 0.1


def negative_terms(queries, neg_block, weight):
    query_sq = jnp.sum(queries * queries, axis=1)
    block_sq = jnp.sum(neg_block * neg_block, axis=1)
    inner_prod = jnp.dot(
        queries, neg_block.T, precision=lax.Precision.HIGHEST, preferred_element_type=jnp.float32
    )
    distance = jnp.sqrt(query_sq[:, None] + block_sq[None, :] - 2.0 * inner_prod + EPSILON)
    coefficient = -jax.nn.sigmoid(MARGIN - distance) / (weight * distance)
    grad_query = queries * jnp.sum(coefficient, axis=1)[:, None] - jnp.dot(
        coefficient, neg_block, precision=lax.Precision.HIGHEST, preferred_element_type=jnp.float32
    )
    grad_block = neg_block * jnp.sum(coefficient, axis=0)[:, None] - jnp.dot(
        coefficient.T, queries, precision=lax.Precision.HIGHEST, preferred_element_type=jnp.float32
    )
    return (grad_query, grad_block)


def send_requests(requests):
    return lax.all_to_all(requests, ("dp", "blk"), split_axis=0, concat_axis=0, tiled=True)


def move_rows(payload):
    return lax.all_to_all(payload, ("dp", "blk"), split_axis=0, concat_axis=0, tiled=True)


def on_device(
    entity_table, adagrad_sum, relations, owner_map, head_ids, rel_ids, tail_ids, neg_ids
):
    dp_count = lax.axis_size("dp")
    blk_count = lax.axis_size("blk")
    owner_count = dp_count * blk_count
    rows_here, width = entity_table.shape
    edge_count = head_ids.shape[0]
    neg_count = neg_ids.shape[0]
    request_count = 2 * edge_count + neg_count
    capacity = max(2, 2 * request_count // owner_count)
    wanted = jnp.concatenate([head_ids, tail_ids, neg_ids])
    position = owner_map[wanted]
    owner_of = position // rows_here
    local_row = position % rows_here
    onehot = (owner_of[:, None] == jnp.arange(owner_count, dtype=jnp.int32)[None, :]).astype(
        jnp.int32
    )
    before = jnp.cumsum(onehot, axis=0) - onehot
    rank_in = jnp.sum(before * onehot, axis=1)
    slot_of = owner_of * capacity + rank_in
    requests = jnp.zeros((owner_count * capacity,), jnp.int32).at[slot_of].set(local_row)
    requests = requests.reshape(owner_count, capacity)
    asked_rows = send_requests(requests)
    served = entity_table[asked_rows]
    fetched = move_rows(served).reshape(owner_count * capacity, width)[slot_of]
    head_rows = fetched[:edge_count]
    tail_rows = fetched[edge_count : 2 * edge_count]
    neg_block = fetched[2 * edge_count :]
    pick = (rel_ids[:, None] == jnp.arange(relations.shape[0], dtype=jnp.int32)[None, :]).astype(
        jnp.float32
    )
    rel_rows = jnp.dot(
        pick, relations, precision=lax.Precision.HIGHEST, preferred_element_type=jnp.float32
    )
    queries = head_rows + rel_rows
    residue = queries - tail_rows
    pos_dist = jnp.sqrt(jnp.sum(residue * residue, axis=1) + EPSILON)
    grad_pos = (jax.nn.sigmoid(pos_dist - MARGIN) / pos_dist)[:, None] * residue
    weight = float(blk_count * neg_count)
    all_queries = lax.all_gather(queries, "blk", axis=0, tiled=True)
    part_query, block_grad = negative_terms(all_queries, neg_block, weight)
    grad_neg = lax.psum_scatter(part_query, "blk", scatter_dimension=0, tiled=True)
    gradients = jnp.concatenate([grad_pos + grad_neg, -grad_pos, block_grad])
    outgoing = jnp.zeros((owner_count * capacity, width), jnp.float32).at[slot_of].set(gradients)
    incoming = move_rows(outgoing.reshape(owner_count, capacity, width))
    summed = (
        jnp.zeros_like(entity_table).at[asked_rows.reshape(-1)].add(incoming.reshape(-1, width))
    )
    new_sum = adagrad_sum + jnp.mean(summed * summed, axis=1)
    new_table = entity_table - LEARNING_RATE * summed / jnp.sqrt(new_sum)[:, None]
    return (new_table, new_sum)


def solution(mesh):
    return jax.shard_map(
        on_device,
        mesh=mesh,
        in_specs=(
            P(("dp", "blk"), None),
            P(("dp", "blk")),
            P(),
            P(),
            P(("dp", "blk")),
            P(("dp", "blk")),
            P(("dp", "blk")),
            P(("dp", "blk")),
        ),
        out_specs=(P(("dp", "blk"), None), P(("dp", "blk"))),
        check_vma=False,
    )
```

```python
import functools

import jax
import jax.numpy as jnp
from jax import lax
from jax.experimental import pallas as pl
from jax.experimental.pallas import tpu as pltpu
from jax.sharding import PartitionSpec as P

MARGIN = 10.0
EPSILON = 1e-05
LEARNING_RATE = 0.1
MESH = pl.DeviceIdType.MESH
F32 = jnp.float32
BF16 = jnp.bfloat16
DEVICES = 128
CAP = 12
PAD = 16
GROUP = 16
CHUNKS = DEVICES // GROUP
SLOTS = GROUP * PAD
LINES = 40
LANES = 128
TAIL = 16


def split(x):
    high = x.astype(BF16)
    return high, (x - high.astype(F32)).astype(BF16)


def dot(a, b, ca, cb):
    return lax.dot_general(a, b, (((ca,), (cb,)), ((), ())), preferred_element_type=F32)


def dot3(a, b, ca, cb):
    return dot(a[0], b[0], ca, cb) + (dot(a[0], b[1], ca, cb) + dot(a[1], b[0], ca, cb))


def iota(shape, axis):
    return lax.broadcasted_iota(jnp.int32, shape, axis)


def onehot(mask):
    return jnp.where(mask, 1.0, 0.0).astype(BF16)


def to_column(row):
    n = row.shape[1]
    return jnp.sum(jnp.where(iota((n, n), 0) == iota((n, n), 1), row, 0.0), axis=1, keepdims=True)


def to_row(column):
    n = column.shape[0]
    return jnp.sum(jnp.where(iota((n, n), 0) == iota((n, n), 1), column, 0.0), axis=0, keepdims=True)


def tail_mask():
    return iota((GROUP, 8, LANES), 1) == iota((GROUP, 8, LANES), 2) // TAIL


def pack(buffer, c, full):
    full = full.reshape(GROUP, PAD, 4 * LANES)
    up, low = full[:, 0:8], full[:, 8:16]
    sub = iota((GROUP, 8, LANES), 1)
    first = sub < 4
    tail_up = jnp.sum(jnp.where(tail_mask(), up[:, :, 3 * LANES :], 0.0), axis=1, keepdims=True)
    tail_low = jnp.sum(
        jnp.where(tail_mask() & first, low[:, :, 3 * LANES :], 0.0), axis=1, keepdims=True
    )
    here = pl.ds(c * GROUP, GROUP)
    for n in range(3):
        buffer[here, 8 * n : 8 * n + 8, :] = up[:, :, LANES * n : LANES * n + LANES]
    buffer[here, 24:32, :] = jnp.where(first, low[:, :, 0:LANES], low[:, :, LANES : 2 * LANES])
    rest = jnp.where(sub == 4, tail_up, jnp.where(sub == 5, tail_low, 0.0))
    buffer[here, 32:40, :] = jnp.where(first, low[:, :, 2 * LANES : 3 * LANES], rest)


def unpack(buffer, c):
    part = buffer[pl.ds(c * GROUP, GROUP)]
    lines = [part[:, 8 * n : 8 * n + 8] for n in range(5)]
    first = iota((GROUP, 8, LANES), 1) < 4
    tail_up = jnp.where(tail_mask(), lines[4][:, 4:5], 0.0)
    tail_low = jnp.where(tail_mask() & first, lines[4][:, 5:6], 0.0)
    turned = pltpu.roll(lines[3].reshape(GROUP * 8, LANES), GROUP * 8 - 4, 0)
    turned = turned.reshape(GROUP, 8, LANES)
    up = jnp.concatenate([lines[0], lines[1], lines[2], tail_up], axis=2)
    low = jnp.concatenate([lines[3], turned, lines[4], tail_low], axis=2)
    return jnp.concatenate([up, low], axis=1).reshape(SLOTS, 4 * LANES)


def step_kernel(
    heads,
    tails,
    negs,
    rels,
    map_hbm,
    table_hbm,
    relations_hbm,
    adagrad,
    table_out,
    sum_out,
    map_ref,
    table,
    relations,
    map_parts,
    table_high,
    table_low,
    ids,
    key_col,
    local_col,
    slot_col,
    slot_row,
    ask_send,
    asked,
    index_col,
    row_send,
    rows,
    wanted,
    rel_rows,
    neg_pieces,
    block_acc,
    coef_cols,
    all_queries,
    part_own,
    part_other,
    part_sibling,
    part_sum,
    part_recv,
    grad_pieces,
    grad_send,
    grads,
    summed,
    load_sem,
    ask_sems,
    row_sems,
    grad_sems,
    query_sems,
    part_sems,
    send_sems,
    query_send_sems,
    part_send_sems,
):
    dp = lax.axis_index("dp")
    blk = lax.axis_index("blk")
    mx, mz = dp // 4, lax.rem(dp, 4)
    my, mc = blk // 2, lax.rem(blk, 2)
    width = table.shape[0]
    body = 3 * LANES
    rows_here = table.shape[1]
    edges = heads.shape[1]

    def deltas(i):
        a, b, c, dc = lax.rem(i, 4), lax.rem(i // 4, 4), lax.rem(i // 16, 4), i // 64
        return a, lax.rem(a + b, 4), lax.rem(a + c, 4), dc

    def ahead(i):
        dx, dy, dz, dc = deltas(i)
        return (
            lax.rem(mx + dx, 4) * 4 + lax.rem(mz + dz, 4),
            lax.rem(my + dy, 4) * 2 + lax.rem(mc + dc, 2),
        )

    def behind(i):
        dx, dy, dz, dc = deltas(i)
        return (
            lax.rem(mx + 4 - dx, 4) * 4 + lax.rem(mz + 4 - dz, 4),
            lax.rem(my + 4 - dy, 4) * 2 + lax.rem(mc + dc, 2),
        )

    def remote(src, dst, send, recv, device):
        return pltpu.make_async_remote_copy(
            src_ref=src,
            dst_ref=dst,
            send_sem=send,
            recv_sem=recv,
            device_id=device,
            device_id_type=MESH,
        )

    load_map = pltpu.make_async_copy(map_hbm, map_ref, load_sem.at[0])
    load_table = pltpu.make_async_copy(table_hbm, table, load_sem.at[1])
    load_relations = pltpu.make_async_copy(relations_hbm, relations, load_sem.at[2])
    load_map.start()
    load_table.start()
    load_relations.start()
    barrier = pltpu.get_barrier_semaphore()

    @pl.loop(1, DEVICES)
    def _(i):
        pl.semaphore_signal(barrier, inc=1, device_id=ahead(i), device_id_type=MESH)

    ids[0:1, :] = heads[...]
    ids[1:2, :] = tails[...]
    ids[2:6, :] = negs[...]
    load_map.wait()
    position_of = map_ref[...]
    map_parts[:, 0:128] = (position_of & 255).astype(F32).astype(BF16)
    map_parts[:, 128:256] = ((position_of >> 8) & 255).astype(F32).astype(BF16)
    map_parts[:, 256:384] = (position_of >> 16).astype(F32).astype(BF16)

    @pl.loop(0, 6)
    def _(t):
        column = to_column(ids[pl.ds(t, 1), :].astype(F32)).astype(jnp.int32)
        line = onehot((column >> 7) == iota((128, map_ref.shape[0]), 1))
        found = dot(line, map_parts[...], 1, 0)
        lane = (column & 127) == iota((128, 128), 1)
        piece = [
            jnp.sum(jnp.where(lane, found[:, 128 * p : 128 * p + 128], 0.0), axis=1, keepdims=True)
            for p in range(3)
        ]
        position = (piece[0] + 256.0 * piece[1] + 65536.0 * piece[2]).astype(jnp.int32)
        owner = position >> 11
        dx = ((owner >> 5) - mx) & 3
        dz = ((owner >> 3) - mz) & 3
        dy = ((owner >> 1) - my) & 3
        dc = (owner - mc) & 1
        key = dc * 64 + ((dz - dx) & 3) * 16 + ((dy - dx) & 3) * 4 + dx
        where = pl.ds(pl.multiple_of(t * 128, 128), 128)
        key_col[where, :] = key.astype(F32)
        local_col[where, :] = (position & (rows_here - 1)).astype(F32)

    count = key_col.shape[0]
    keys = key_col[...]
    key_hot = onehot(keys.astype(jnp.int32) == iota((count, DEVICES), 1))
    earlier = onehot(iota((count, count), 1) < iota((count, count), 0))
    before = dot(earlier, key_hot, 1, 0)
    rank = jnp.sum(before * key_hot.astype(F32), axis=1, keepdims=True)
    local = local_col[...].astype(jnp.int32)
    place = rank.astype(jnp.int32)
    lane = iota((count, LANES), 1)
    spot = (place == lane) | ((place >= 8) & (place + 4 == lane))
    upper = jnp.where(spot, (local >> 8).astype(F32), 0.0).astype(BF16)
    lower = jnp.where(spot, (local & 255).astype(F32), 0.0).astype(BF16)
    asks = 256.0 * dot(key_hot, upper, 0, 0) + dot(key_hot, lower, 0, 0)
    ask_send[...] = asks.reshape(DEVICES, 1, 128)
    slot = keys * float(PAD) + rank
    slot_col[...] = slot
    for t in range(6):
        slot_row[t : t + 1, :] = to_row(slot[128 * t : 128 * t + 128])

    load_table.wait()
    high, low = split(table[...])
    table_high[0:width] = high
    table_low[0:width] = low
    for j in range(1, LANES // TAIL):
        table_high[body + TAIL * j : body + TAIL * j + TAIL] = high[body:]
        table_low[body + TAIL * j : body + TAIL * j + TAIL] = low[body:]
    summed[...] = jnp.zeros_like(summed)
    wanted[...] = jnp.zeros_like(wanted)
    asked[0] = ask_send[0]

    pl.semaphore_wait(barrier, DEVICES - 1)

    def ask_copy(i):
        return remote(
            ask_send.at[i], asked.at[i], send_sems.at[0], ask_sems.at[i // GROUP], ahead(i)
        )

    @pl.loop(1, DEVICES)
    def _(i):
        ask_copy(i).start()

    def wait_chunk(buffer, sems, c):
        @pl.when(c == 0)
        def _():
            part = buffer.at[pl.ds(1, GROUP - 1)]
            pltpu.make_async_copy(part, part, sems.at[0]).wait()

        @pl.when(c > 0)
        def _():
            part = buffer.at[pl.ds(c * GROUP, GROUP)]
            pltpu.make_async_copy(part, part, sems.at[c]).wait()

    def row_copy(i):
        return remote(
            row_send.at[i],
            rows.at[i],
            send_sems.at[1],
            row_sems.at[i // GROUP],
            behind(i),
        )

    @pl.loop(0, CHUNKS)
    def _(c):
        wait_chunk(asked, ask_sems, c)
        part = jnp.broadcast_to(asked[pl.ds(c * GROUP, GROUP)], (GROUP, PAD, 128))
        part = part.reshape(SLOTS, 128)
        index = jnp.sum(
            jnp.where(lax.rem(iota((SLOTS, 128), 0), PAD) == iota((SLOTS, 128), 1), part, 0.0),
            axis=1,
            keepdims=True,
        )
        index_col[pl.ds(pl.multiple_of(c * SLOTS, SLOTS), SLOTS), :] = index
        pick = onehot(index.astype(jnp.int32) == iota((SLOTS, rows_here), 1))
        picked = dot(pick, table_high[...], 1, 1) + dot(pick, table_low[...], 1, 1)
        pack(row_send, c, picked)

        @pl.when(c == 0)
        def _():
            rows[0] = row_send[0]

        @pl.loop(0, GROUP)
        def _(g):
            @pl.when(c * GROUP + g > 0)
            def _():
                row_copy(c * GROUP + g).start()

    load_relations.wait()
    rel_column = to_column(rels[...].astype(F32)).astype(jnp.int32)
    rel_rows[...] = jnp.zeros_like(rel_rows)

    @pl.loop(0, relations.shape[1] // 256)
    def _(t):
        high, low = split(relations[:, pl.ds(pl.multiple_of(t * 256, 256), 256)])
        pick = onehot(rel_column - t * 256 == iota((edges, 256), 1))
        rel_rows[:, 0:width] += dot(pick, high, 1, 1) + dot(pick, low, 1, 1)

    @pl.loop(0, CHUNKS)
    def _(c):
        wait_chunk(rows, row_sems, c)
        high, low = split(unpack(rows, c))
        place = onehot(slot_col[...].astype(jnp.int32) - c * SLOTS == iota((count, SLOTS), 1))
        wanted[...] += dot(place, high, 1, 0) + dot(place, low, 1, 0)

    high, low = split(wanted[:, body:])
    fold = onehot(lax.rem(iota((LANES, LANES), 0), TAIL) == iota((LANES, LANES), 1))
    wanted[:, body:] = dot(high, fold, 1, 0) + dot(low, fold, 1, 0)
    queries = wanted[0:edges, :] + rel_rows[...]
    residue = queries - wanted[edges : 2 * edges, :]
    pos_dist = jnp.sqrt(jnp.sum(residue * residue, axis=1, keepdims=True) + EPSILON)
    grad_pos = (1.0 / (1.0 + jnp.exp(MARGIN - pos_dist)) / pos_dist) * residue
    all_queries[0, 0] = queries

    sibling = (dp, blk + 1 - 2 * mc)

    def query_copy(dy):
        return remote(
            all_queries.at[0, 0],
            all_queries.at[dy, 0],
            query_send_sems.at[dy, 0],
            query_sems.at[dy, 0],
            (dp, lax.rem(my + dy, 4) * 2 + mc),
        )

    def forward_copy(dy):
        return remote(
            all_queries.at[dy, 0],
            all_queries.at[dy, 1],
            query_send_sems.at[dy, 1],
            query_sems.at[dy, 1],
            sibling,
        )

    for dy in (1, 3, 2):
        query_copy(dy).start()

    negatives = wanted[2 * edges :, :]
    high, low = split(negatives)
    neg_pieces[0] = high
    neg_pieces[1] = low
    neg_col = jnp.sum(negatives * negatives, axis=1, keepdims=True)
    neg_count = negatives.shape[0]
    neg_sq = jnp.concatenate(
        [to_row(neg_col[128 * t : 128 * t + 128]) for t in range(neg_count // 128)], axis=1
    )
    block_acc[...] = jnp.zeros_like(block_acc)
    coef_cols[...] = jnp.zeros_like(coef_cols)
    weight = 8.0 * neg_count

    def order(t):
        return t + (t // 2) * (1 - 2 * lax.rem(t, 2))

    def sibling_copy(dy):
        return remote(
            part_other.at[dy],
            part_sibling.at[dy],
            part_send_sems.at[dy, 0],
            part_sems.at[dy, 0],
            sibling,
        )

    def home_copy(dy):
        return remote(
            part_sum.at[dy],
            part_recv.at[dy],
            part_send_sems.at[dy, 1],
            part_sems.at[dy, 1],
            (dp, lax.rem(my + 4 - dy, 4) * 2 + mc),
        )

    def block_terms(block):
        pieces = split(block)
        block_sq = jnp.sum(block * block, axis=1, keepdims=True)
        neg_parts = (neg_pieces[0], neg_pieces[1])
        inner = dot3(pieces, neg_parts, 1, 1)
        dist = jnp.sqrt(block_sq + neg_sq - 2.0 * inner + EPSILON)
        coef = -1.0 / ((1.0 + jnp.exp(dist - MARGIN)) * (weight * dist))
        coef_parts = split(coef)
        coef_cols[...] += jnp.sum(coef, axis=0, keepdims=True)
        block_acc[...] += dot3(coef_parts, pieces, 0, 0)
        return block * jnp.sum(coef, axis=1, keepdims=True) - dot3(coef_parts, neg_parts, 1, 0)

    def finish(dy):
        sibling_copy(dy).wait_recv()
        part_sum[dy] = part_own[dy] + part_sibling[dy]

    @pl.loop(0, 4)
    def _(t):
        dy = order(t)

        @pl.when(t > 0)
        def _():
            query_copy(dy).wait_recv()

        forward_copy(dy).start()
        part_own[dy] = block_terms(all_queries[dy, 0])
        forward_copy(dy).wait_recv()
        part_other[dy] = block_terms(all_queries[dy, 1])
        sibling_copy(dy).start()

        @pl.when(t > 1)
        def _():
            last = order(t - 1)
            finish(last)
            home_copy(last).start()

    finish(2)
    home_copy(2).start()
    finish(0)
    for dy in (1, 3, 2):
        home_copy(dy).wait_recv()
    grad_neg = (part_sum[0] + part_recv[1]) + (part_recv[2] + part_recv[3])
    high, low = split(grad_pos + grad_neg)
    grad_pieces[0, 0:edges] = high
    grad_pieces[1, 0:edges] = low
    high, low = split(-grad_pos)
    grad_pieces[0, edges : 2 * edges] = high
    grad_pieces[1, edges : 2 * edges] = low
    coef_col = jnp.concatenate(
        [to_column(coef_cols[:, 128 * t : 128 * t + 128]) for t in range(neg_count // 128)], axis=0
    )
    high, low = split(wanted[2 * edges :, :] * coef_col - block_acc[...])
    grad_pieces[0, 2 * edges :] = high
    grad_pieces[1, 2 * edges :] = low

    spread = onehot(iota((LANES, LANES), 0) == lax.rem(iota((LANES, LANES), 1), TAIL))
    for n in range(2):
        grad_pieces[n, :, body:] = dot(grad_pieces[n, :, body:], spread, 1, 0).astype(BF16)

    def grad_copy(i):
        return remote(
            grad_send.at[i],
            grads.at[i],
            send_sems.at[2],
            grad_sems.at[i // GROUP],
            ahead(i),
        )

    @pl.loop(0, CHUNKS)
    def _(c):
        line = iota((SLOTS, LANES), 0)
        base = line + c * SLOTS - jnp.where(lax.rem(line, PAD) < CAP, 0, PAD - CAP)
        place = jnp.concatenate(
            [onehot(slot_row[t : t + 1, :].astype(jnp.int32) == base) for t in range(6)], axis=1
        )
        packed = dot(place, grad_pieces[0], 1, 0) + dot(place, grad_pieces[1], 1, 0)
        pack(grad_send, c, packed)

        @pl.when(c == 0)
        def _():
            grads[0] = grad_send[0]

        @pl.loop(0, GROUP)
        def _(g):
            @pl.when(c * GROUP + g > 0)
            def _():
                grad_copy(c * GROUP + g).start()

    @pl.loop(0, CHUNKS)
    def _(c):
        wait_chunk(grads, grad_sems, c)
        high, low = split(unpack(grads, c).T)
        index = index_col[pl.ds(pl.multiple_of(c * SLOTS, SLOTS), SLOTS), :].astype(jnp.int32)
        used = lax.rem(iota((SLOTS, 1), 0), PAD) < CAP
        pick = onehot(jnp.where(used, index, -1) == iota((SLOTS, rows_here), 1))
        summed[...] += dot(high, pick, 1, 0) + dot(low, pick, 1, 0)

    tail = summed[body:width]
    for j in range(1, LANES // TAIL):
        tail = tail + summed[body + TAIL * j : body + TAIL * j + TAIL]
    total = jnp.concatenate([summed[0:body], tail], axis=0)
    new_sum = adagrad[...] + jnp.sum(total * total, axis=0, keepdims=True) * (1.0 / width)
    sum_out[...] = new_sum
    table_out[...] = table[...] - total * (LEARNING_RATE / jnp.sqrt(new_sum))

    part = ask_send.at[pl.ds(1, DEVICES - 1)]
    pltpu.make_async_copy(part, part, send_sems.at[0]).wait()
    for n, buffer in ((1, row_send), (2, grad_send)):
        part = buffer.at[pl.ds(1, DEVICES - 1)]
        pltpu.make_async_copy(part, part, send_sems.at[n]).wait()
    for dy in range(4):
        forward_copy(dy).wait_send()
        sibling_copy(dy).wait_send()
        if dy > 0:
            query_copy(dy).wait_send()
            home_copy(dy).wait_send()


def on_device(entity_table, adagrad_sum, relations, owner_map, head_ids, rel_ids, tail_ids, neg_ids):
    rows_here, width = entity_table.shape
    edges = head_ids.shape[0]
    neg_count = neg_ids.shape[0]
    count = 2 * edges + neg_count
    map_rows = owner_map.shape[0] // 128
    vmem = pl.BlockSpec(memory_space=pltpu.VMEM)
    hbm = pl.BlockSpec(memory_space=pl.ANY)
    wide = 4 * LANES
    slots = pltpu.VMEM((DEVICES, LINES, LANES), F32)
    parts = pltpu.VMEM((4, edges, wide), F32)
    sem = pltpu.SemaphoreType.DMA
    new_table, new_sum = pl.pallas_call(
        step_kernel,
        out_shape=(
            jax.ShapeDtypeStruct((width, rows_here), F32),
            jax.ShapeDtypeStruct((1, rows_here), F32),
        ),
        in_specs=[vmem, vmem, vmem, vmem, hbm, hbm, hbm, vmem],
        out_specs=(vmem, vmem),
        scratch_shapes=[
            pltpu.VMEM((map_rows, 128), jnp.int32),
            pltpu.VMEM((width, rows_here), F32),
            pltpu.VMEM((width, relations.shape[0]), F32),
            pltpu.VMEM((map_rows, 384), BF16),
            pltpu.VMEM((wide, rows_here), BF16),
            pltpu.VMEM((wide, rows_here), BF16),
            pltpu.VMEM((8, 128), jnp.int32),
            pltpu.VMEM((count, 1), F32),
            pltpu.VMEM((count, 1), F32),
            pltpu.VMEM((count, 1), F32),
            pltpu.VMEM((8, 128), F32),
            pltpu.VMEM((DEVICES, 1, 128), F32),
            pltpu.VMEM((DEVICES, 1, 128), F32),
            pltpu.VMEM((DEVICES * PAD, 1), F32),
            slots,
            slots,
            pltpu.VMEM((count, wide), F32),
            pltpu.VMEM((edges, wide), F32),
            pltpu.VMEM((2, neg_count, wide), BF16),
            pltpu.VMEM((neg_count, wide), F32),
            pltpu.VMEM((1, neg_count), F32),
            pltpu.VMEM((4, 2, edges, wide), F32),
            parts,
            parts,
            parts,
            parts,
            parts,
            pltpu.VMEM((2, count, wide), BF16),
            slots,
            slots,
            pltpu.VMEM((wide, rows_here), F32),
            sem((3,)),
            sem((CHUNKS,)),
            sem((CHUNKS,)),
            sem((CHUNKS,)),
            sem((4, 2)),
            sem((4, 2)),
            sem((3,)),
            sem((4, 2)),
            sem((4, 2)),
        ],
        compiler_params=pltpu.CompilerParams(
            collective_id=0, has_side_effects=True, vmem_limit_bytes=64000000
        ),
    )(
        head_ids.reshape(1, edges),
        tail_ids.reshape(1, edges),
        neg_ids.reshape(neg_count // 128, 128),
        rel_ids.reshape(1, edges),
        owner_map.reshape(map_rows, 128),
        entity_table.T,
        relations.T,
        adagrad_sum.reshape(1, rows_here),
    )
    return new_table.T, new_sum.reshape(rows_here)


def solution(mesh):
    assert dict(mesh.shape) == {"dp": 16, "blk": 8}
    return jax.shard_map(
        on_device,
        mesh=mesh,
        in_specs=(
            P(("dp", "blk"), None),
            P(("dp", "blk")),
            P(),
            P(),
            P(("dp", "blk")),
            P(("dp", "blk")),
            P(("dp", "blk")),
            P(("dp", "blk")),
        ),
        out_specs=(P(("dp", "blk"), None), P(("dp", "blk"))),
        check_vma=False,
    )
```

```python
import functools

import jax
import jax.numpy as jnp
from jax import lax
from jax.experimental import pallas as pl
from jax.experimental.pallas import tpu as pltpu
from jax.sharding import PartitionSpec as P

MARGIN = 10.0
EPSILON = 1e-05
LEARNING_RATE = 0.1
MESH = pl.DeviceIdType.MESH
F32 = jnp.float32
BF16 = jnp.bfloat16
DEVICES = 128
CAP = 12
PAD = 16
GROUP = 16
CHUNKS = DEVICES // GROUP
SLOTS = GROUP * PAD
LINES = 40
LIMIT = 48 * 1024 * 1024
LANES = 128
TAIL = 16
REL = 256
REL_PARTS = 3


def split(x):
    high = x.astype(BF16)
    return high, (x - high.astype(F32)).astype(BF16)


def dot(a, b, ca, cb):
    return lax.dot_general(a, b, (((ca,), (cb,)), ((), ())), preferred_element_type=F32)


def dot3(a, b, ca, cb):
    return dot(a[0], b[0], ca, cb) + (dot(a[0], b[1], ca, cb) + dot(a[1], b[0], ca, cb))


def iota(shape, axis):
    return lax.broadcasted_iota(jnp.int32, shape, axis)


def onehot(mask):
    return jnp.where(mask, 1.0, 0.0).astype(BF16)


def to_column(row):
    n = row.shape[1]
    return jnp.sum(jnp.where(iota((n, n), 0) == iota((n, n), 1), row, 0.0), axis=1, keepdims=True)


def to_row(column):
    n = column.shape[0]
    return jnp.sum(jnp.where(iota((n, n), 0) == iota((n, n), 1), column, 0.0), axis=0, keepdims=True)


def tail_mask():
    return iota((GROUP, 8, LANES), 1) == iota((GROUP, 8, LANES), 2) // TAIL


def pack(buffer, c, full):
    full = full.reshape(GROUP, PAD, 4 * LANES)
    up, low = full[:, 0:8], full[:, 8:16]
    sub = iota((GROUP, 8, LANES), 1)
    first = sub < 4
    tail_up = jnp.sum(jnp.where(tail_mask(), up[:, :, 3 * LANES :], 0.0), axis=1, keepdims=True)
    tail_low = jnp.sum(
        jnp.where(tail_mask() & first, low[:, :, 3 * LANES :], 0.0), axis=1, keepdims=True
    )
    here = pl.ds(c * GROUP, GROUP)
    for n in range(3):
        buffer[here, 8 * n : 8 * n + 8, :] = up[:, :, LANES * n : LANES * n + LANES]
    buffer[here, 24:32, :] = jnp.where(first, low[:, :, 0:LANES], low[:, :, LANES : 2 * LANES])
    rest = jnp.where(sub == 4, tail_up, jnp.where(sub == 5, tail_low, 0.0))
    buffer[here, 32:40, :] = jnp.where(first, low[:, :, 2 * LANES : 3 * LANES], rest)


def unpack(buffer, c):
    part = buffer[pl.ds(c * GROUP, GROUP)]
    lines = [part[:, 8 * n : 8 * n + 8] for n in range(5)]
    first = iota((GROUP, 8, LANES), 1) < 4
    tail_up = jnp.where(tail_mask(), lines[4][:, 4:5], 0.0)
    tail_low = jnp.where(tail_mask() & first, lines[4][:, 5:6], 0.0)
    turned = pltpu.roll(lines[3].reshape(GROUP * 8, LANES), GROUP * 8 - 4, 0)
    turned = turned.reshape(GROUP, 8, LANES)
    up = jnp.concatenate([lines[0], lines[1], lines[2], tail_up], axis=2)
    low = jnp.concatenate([lines[3], turned, lines[4], tail_low], axis=2)
    return jnp.concatenate([up, low], axis=1).reshape(SLOTS, 4 * LANES)


def to_lines(x):
    tail = x[:, 3 * LANES :]
    for shift in (TAIL, 2 * TAIL, 4 * TAIL):
        tail = tail + pltpu.roll(tail, shift, 1)
    tail = tail.reshape(GROUP, 8, LANES)
    tail = jnp.sum(jnp.where(tail_mask(), tail, 0.0), axis=1)
    return jnp.concatenate([x[:, LANES * n : LANES * n + LANES] for n in range(3)] + [tail], axis=0)


def from_lines(lines):
    tail = lines[3 * LANES :].reshape(GROUP, 1, LANES)
    tail = jnp.where(tail_mask(), tail, 0.0).reshape(LANES, LANES)
    for shift in (4 * TAIL, 2 * TAIL, TAIL):
        tail = tail + pltpu.roll(tail, shift, 1)
    tail = jnp.where(iota((LANES, LANES), 1) < TAIL, tail, 0.0)
    return jnp.concatenate([lines[LANES * n : LANES * n + LANES] for n in range(3)] + [tail], axis=1)


def step_kernel(
    heads,
    tails,
    negs,
    rels,
    map_hbm,
    table_hbm,
    relations_hbm,
    adagrad,
    table_out,
    sum_out,
    map_ref,
    table,
    relations,
    map_parts,
    table_high,
    table_low,
    ids,
    key_col,
    ask_col,
    local_col,
    slot_col,
    slot_row,
    ask_send,
    ask_mid,
    ask_sum,
    asked,
    index_col,
    row_send,
    rows,
    wanted,
    rel_acc,
    rel_rows,
    neg_pieces,
    block_acc,
    coef_cols,
    all_queries,
    part_own,
    part_other,
    part_sibling,
    part_sum,
    part_recv,
    grad_pieces,
    grad_send,
    grads,
    summed,
    load_sem,
    ask_sems,
    row_sems,
    grad_sems,
    query_sems,
    part_sems,
    send_sems,
    query_send_sems,
    part_send_sems,
):
    dp = lax.axis_index("dp")
    blk = lax.axis_index("blk")
    mx, mz = dp // 4, lax.rem(dp, 4)
    my, mc = blk // 2, lax.rem(blk, 2)
    width = table.shape[0]
    body = 3 * LANES
    rows_here = table.shape[1]
    edges = heads.shape[1]
    rel_chunks = relations_hbm.shape[1] // REL
    rel_step = relations.shape[1] // REL
    rel_cuts = [min(n * rel_step, rel_chunks) for n in range(REL_PARTS + 1)]

    def deltas(i):
        a, b, c, dc = lax.rem(i, 4), lax.rem(i // 4, 4), lax.rem(i // 16, 4), i // 64
        return a, lax.rem(a + b, 4), lax.rem(a + c, 4), dc

    def ahead(i):
        dx, dy, dz, dc = deltas(i)
        return (
            lax.rem(mx + dx, 4) * 4 + lax.rem(mz + dz, 4),
            lax.rem(my + dy, 4) * 2 + lax.rem(mc + dc, 2),
        )

    def behind(i):
        dx, dy, dz, dc = deltas(i)
        return (
            lax.rem(mx + 4 - dx, 4) * 4 + lax.rem(mz + 4 - dz, 4),
            lax.rem(my + 4 - dy, 4) * 2 + lax.rem(mc + dc, 2),
        )

    def remote(src, dst, send, recv, device):
        return pltpu.make_async_remote_copy(
            src_ref=src,
            dst_ref=dst,
            send_sem=send,
            recv_sem=recv,
            device_id=device,
            device_id_type=MESH,
        )

    load_map = pltpu.make_async_copy(map_hbm, map_ref, load_sem.at[0])
    load_table = pltpu.make_async_copy(table_hbm, table, load_sem.at[1])

    def load_relations(half):
        first, lanes = rel_cuts[half] * REL, (rel_cuts[half + 1] - rel_cuts[half]) * REL
        part = relations_hbm.at[:, pl.ds(first, lanes)]
        return pltpu.make_async_copy(part, relations.at[:, pl.ds(0, lanes)], load_sem.at[2])

    load_map.start()
    load_table.start()
    load_relations(0).start()
    barrier = pltpu.get_barrier_semaphore()

    def in_group(r):
        return dp, lax.rem(my + lax.rem(r, 4), 4) * 2 + lax.rem(mc + r // 4, 2)

    def in_plane(p):
        return lax.rem(mx + p // 4, 4) * 4 + lax.rem(mz + lax.rem(p, 4), 4), blk

    @pl.loop(1, 8)
    def _(r):
        pl.semaphore_signal(barrier, inc=1, device_id=in_group(r), device_id_type=MESH)

    @pl.loop(1, 16)
    def _(p):
        pl.semaphore_signal(barrier, inc=1, device_id=in_plane(p), device_id_type=MESH)

    ids[0:1, :] = heads[...]
    ids[1:2, :] = tails[...]
    ids[2:6, :] = negs[...]
    load_map.wait()
    position_of = map_ref[...]
    map_parts[:, 0:128] = (position_of & 255).astype(F32).astype(BF16)
    map_parts[:, 128:256] = ((position_of >> 8) & 255).astype(F32).astype(BF16)
    map_parts[:, 256:384] = (position_of >> 16).astype(F32).astype(BF16)

    @pl.loop(0, 6)
    def _(t):
        column = to_column(ids[pl.ds(t, 1), :].astype(F32)).astype(jnp.int32)
        line = onehot((column >> 7) == iota((128, map_ref.shape[0]), 1))
        found = dot(line, map_parts[...], 1, 0)
        lane = (column & 127) == iota((128, 128), 1)
        piece = [
            jnp.sum(jnp.where(lane, found[:, 128 * p : 128 * p + 128], 0.0), axis=1, keepdims=True)
            for p in range(3)
        ]
        position = (piece[0] + 256.0 * piece[1] + 65536.0 * piece[2]).astype(jnp.int32)
        owner = position >> 11
        dx = ((owner >> 5) - mx) & 3
        dz = ((owner >> 3) - mz) & 3
        dy = ((owner >> 1) - my) & 3
        dc = (owner - mc) & 1
        key = dc * 64 + ((dz - dx) & 3) * 16 + ((dy - dx) & 3) * 4 + dx
        ask = (dc * 4 + dy) * 16 + dx * 4 + dz
        where = pl.ds(pl.multiple_of(t * 128, 128), 128)
        key_col[where, :] = key.astype(F32)
        ask_col[where, :] = ask.astype(F32)
        local_col[where, :] = (position & (rows_here - 1)).astype(F32)

    count = key_col.shape[0]
    keys = key_col[...]
    key_hot = onehot(ask_col[...].astype(jnp.int32) == iota((count, DEVICES), 1))
    earlier = onehot(iota((count, count), 1) < iota((count, count), 0))
    before = dot(earlier, key_hot, 1, 0)
    rank = jnp.sum(before * key_hot.astype(F32), axis=1, keepdims=True)
    local = local_col[...].astype(jnp.int32)
    place = rank.astype(jnp.int32)
    lane = iota((count, LANES), 1)
    spread = lane - (ask_col[...].astype(jnp.int32) // 16) * PAD
    spot = (place == spread) | ((place >= 8) & (place + 4 == spread))
    upper = jnp.where(spot, (local >> 8).astype(F32), 0.0).astype(BF16)
    lower = jnp.where(spot, (local & 255).astype(F32), 0.0).astype(BF16)
    asks = 256.0 * dot(key_hot, upper, 0, 0) + dot(key_hot, lower, 0, 0)
    ask_send[...] = asks.reshape(8, 16, 1, LANES)
    slot = keys * float(PAD) + rank
    slot_col[...] = slot
    for t in range(6):
        slot_row[t : t + 1, :] = to_row(slot[128 * t : 128 * t + 128])

    load_table.wait()
    high, low = split(table[...])
    table_high[0:width] = high
    table_low[0:width] = low
    for j in range(1, LANES // TAIL):
        table_high[body + TAIL * j : body + TAIL * j + TAIL] = high[body:]
        table_low[body + TAIL * j : body + TAIL * j + TAIL] = low[body:]
    summed[...] = jnp.zeros_like(summed)
    wanted[...] = jnp.zeros_like(wanted)
    ask_mid[0] = ask_send[0]

    pl.semaphore_wait(barrier, 22)

    def group_ask(r):
        return remote(ask_send.at[r], ask_mid.at[r], send_sems.at[0], ask_sems.at[0], in_group(r))

    def plane_ask(p):
        return remote(ask_sum.at[p], asked.at[p], send_sems.at[3], ask_sems.at[1], in_plane(p))

    @pl.loop(1, 8)
    def _(r):
        group_ask(r).start()

    part = ask_mid.at[pl.ds(1, 7)]
    pltpu.make_async_copy(part, part, ask_sems.at[0]).wait()
    ask_sum[...] = jnp.sum(ask_mid[...], axis=0)

    @pl.loop(1, 16)
    def _(p):
        plane_ask(p).start()

    asked[0] = ask_sum[0]
    part = asked.at[pl.ds(1, 15)]
    pltpu.make_async_copy(part, part, ask_sems.at[1]).wait()

    def wait_chunk(buffer, sems, c):
        @pl.when(c == 0)
        def _():
            part = buffer.at[pl.ds(1, GROUP - 1)]
            pltpu.make_async_copy(part, part, sems.at[0]).wait()

        @pl.when(c > 0)
        def _():
            part = buffer.at[pl.ds(c * GROUP, GROUP)]
            pltpu.make_async_copy(part, part, sems.at[c]).wait()

    def row_copy(i):
        return remote(
            row_send.at[i],
            rows.at[i],
            send_sems.at[1],
            row_sems.at[i // GROUP],
            behind(i),
        )

    @pl.loop(0, CHUNKS)
    def _(c):
        parts = []
        for g in range(GROUP):
            dx, dy, dz, dc = deltas(c * GROUP + g)
            line = jnp.broadcast_to(asked[dx * 4 + dz], (PAD, LANES))
            lane = iota((PAD, LANES), 1) - (dc * 4 + dy) * PAD
            parts.append(jnp.where(lane == iota((PAD, LANES), 0), line, 0.0))
        index = jnp.sum(jnp.concatenate(parts, axis=0), axis=1, keepdims=True)
        index_col[pl.ds(pl.multiple_of(c * SLOTS, SLOTS), SLOTS), :] = index
        pick = onehot(index.astype(jnp.int32) == iota((SLOTS, rows_here), 1))
        picked = dot(pick, table_high[...], 1, 1) + dot(pick, table_low[...], 1, 1)
        pack(row_send, c, picked)

        @pl.when(c == 0)
        def _():
            rows[0] = row_send[0]

        @pl.loop(0, GROUP)
        def _(g):
            @pl.when(c * GROUP + g > 0)
            def _():
                row_copy(c * GROUP + g).start()

    rel_acc[...] = jnp.zeros_like(rel_acc)
    for half in range(REL_PARTS):
        load_relations(half).wait()

        @pl.loop(0, rel_cuts[half + 1] - rel_cuts[half])
        def _(t):
            high, low = split(relations[:, pl.ds(pl.multiple_of(t * REL, REL), REL)])
            base = (t + rel_cuts[half]) * REL
            pick = onehot(iota((REL, edges), 0) + base == rels[...])
            found = dot(jnp.concatenate([high, low], axis=0), pick, 1, 0)
            rel_acc[...] += found[0:width] + found[width:]

        if half + 1 < REL_PARTS:
            load_relations(half + 1).start()

    rel_rows[...] = jnp.zeros_like(rel_rows)
    rel_rows[:, 0:width] = rel_acc[...].T

    @pl.loop(0, CHUNKS)
    def _(c):
        wait_chunk(rows, row_sems, c)
        high, low = split(unpack(rows, c))
        place = onehot(slot_col[...].astype(jnp.int32) - c * SLOTS == iota((count, SLOTS), 1))
        wanted[...] += dot(place, high, 1, 0) + dot(place, low, 1, 0)

    high, low = split(wanted[:, body:])
    fold = onehot(lax.rem(iota((LANES, LANES), 0), TAIL) == iota((LANES, LANES), 1))
    wanted[:, body:] = dot(high, fold, 1, 0) + dot(low, fold, 1, 0)
    queries = wanted[0:edges, :] + rel_rows[...]
    residue = queries - wanted[edges : 2 * edges, :]
    pos_dist = jnp.sqrt(jnp.sum(residue * residue, axis=1, keepdims=True) + EPSILON)
    grad_pos = (1.0 / (1.0 + jnp.exp(MARGIN - pos_dist)) / pos_dist) * residue
    all_queries[0, 0] = to_lines(queries)

    sibling = (dp, blk + 1 - 2 * mc)

    def query_copy(dy):
        return remote(
            all_queries.at[0, 0],
            all_queries.at[dy, 0],
            query_send_sems.at[dy, 0],
            query_sems.at[dy, 0],
            (dp, lax.rem(my + dy, 4) * 2 + mc),
        )

    def forward_copy(dy):
        return remote(
            all_queries.at[dy, 0],
            all_queries.at[dy, 1],
            query_send_sems.at[dy, 1],
            query_sems.at[dy, 1],
            sibling,
        )

    query_copy(1).start()
    query_copy(3).start()
    forward_copy(0).start()
    negatives = wanted[2 * edges :, :]
    high, low = split(negatives)
    neg_pieces[0] = high
    neg_pieces[1] = low
    neg_col = jnp.sum(negatives * negatives, axis=1, keepdims=True)
    neg_count = negatives.shape[0]
    neg_sq = jnp.concatenate(
        [to_row(neg_col[128 * t : 128 * t + 128]) for t in range(neg_count // 128)], axis=1
    )
    block_acc[...] = jnp.zeros_like(block_acc)
    coef_cols[...] = jnp.zeros_like(coef_cols)
    weight = 8.0 * neg_count

    def order(t):
        return t + (t // 2) * (1 - 2 * lax.rem(t, 2))

    def sibling_copy(dy):
        return remote(
            part_other.at[dy],
            part_sibling.at[dy],
            part_send_sems.at[dy, 0],
            part_sems.at[dy, 0],
            sibling,
        )

    def home_copy(dy):
        return remote(
            part_sum.at[dy],
            part_recv.at[dy],
            part_send_sems.at[dy, 1],
            part_sems.at[dy, 1],
            (dp, lax.rem(my + 4 - dy, 4) * 2 + mc),
        )

    def block_terms(block):
        pieces = split(block)
        block_sq = jnp.sum(block * block, axis=1, keepdims=True)
        neg_parts = (neg_pieces[0], neg_pieces[1])
        inner = dot3(pieces, neg_parts, 1, 1)
        dist = jnp.sqrt(block_sq + neg_sq - 2.0 * inner + EPSILON)
        coef = -1.0 / ((1.0 + jnp.exp(dist - MARGIN)) * (weight * dist))
        coef_parts = split(coef)
        coef_cols[...] += jnp.sum(coef, axis=0, keepdims=True)
        block_acc[...] += dot3(coef_parts, pieces, 0, 0)
        return block * jnp.sum(coef, axis=1, keepdims=True) - dot3(coef_parts, neg_parts, 1, 0)

    def finish(dy):
        sibling_copy(dy).wait_recv()
        part_sum[dy] = part_own[dy] + part_sibling[dy]

    @pl.loop(0, 4)
    def _(t):
        dy = order(t)

        @pl.when(t == 1)
        def _():
            query_copy(1).wait_recv()
            forward_copy(1).start()
            query_copy(3).wait_recv()
            query_copy(2).start()
            forward_copy(3).start()

        @pl.when(t == 3)
        def _():
            query_copy(2).wait_recv()
            forward_copy(2).start()

        part_own[dy] = to_lines(block_terms(from_lines(all_queries[dy, 0])))
        forward_copy(dy).wait_recv()
        part_other[dy] = to_lines(block_terms(from_lines(all_queries[dy, 1])))
        sibling_copy(dy).start()

        @pl.when(t > 1)
        def _():
            last = order(t - 1)
            finish(last)
            home_copy(last).start()

    finish(2)
    home_copy(2).start()
    finish(0)
    for dy in (1, 3, 2):
        home_copy(dy).wait_recv()
    grad_neg = from_lines((part_sum[0] + part_recv[1]) + (part_recv[2] + part_recv[3]))
    high, low = split(grad_pos + grad_neg)
    grad_pieces[0, 0:edges] = high
    grad_pieces[1, 0:edges] = low
    high, low = split(-grad_pos)
    grad_pieces[0, edges : 2 * edges] = high
    grad_pieces[1, edges : 2 * edges] = low
    coef_col = jnp.concatenate(
        [to_column(coef_cols[:, 128 * t : 128 * t + 128]) for t in range(neg_count // 128)], axis=0
    )
    high, low = split(wanted[2 * edges :, :] * coef_col - block_acc[...])
    grad_pieces[0, 2 * edges :] = high
    grad_pieces[1, 2 * edges :] = low

    spread = onehot(iota((LANES, LANES), 0) == lax.rem(iota((LANES, LANES), 1), TAIL))
    for n in range(2):
        grad_pieces[n, :, body:] = dot(grad_pieces[n, :, body:], spread, 1, 0).astype(BF16)

    def grad_copy(i):
        return remote(
            grad_send.at[i],
            grads.at[i],
            send_sems.at[2],
            grad_sems.at[i // GROUP],
            ahead(i),
        )

    @pl.loop(0, CHUNKS)
    def _(c):
        line = iota((SLOTS, LANES), 0)
        base = line + c * SLOTS - jnp.where(lax.rem(line, PAD) < CAP, 0, PAD - CAP)
        place = jnp.concatenate(
            [onehot(slot_row[t : t + 1, :].astype(jnp.int32) == base) for t in range(6)], axis=1
        )
        packed = dot(place, grad_pieces[0], 1, 0) + dot(place, grad_pieces[1], 1, 0)
        pack(grad_send, c, packed)

        @pl.when(c == 0)
        def _():
            grads[0] = grad_send[0]

        @pl.loop(0, GROUP)
        def _(g):
            @pl.when(c * GROUP + g > 0)
            def _():
                grad_copy(c * GROUP + g).start()

    @pl.loop(0, CHUNKS)
    def _(c):
        wait_chunk(grads, grad_sems, c)
        high, low = split(unpack(grads, c).T)
        index = index_col[pl.ds(pl.multiple_of(c * SLOTS, SLOTS), SLOTS), :].astype(jnp.int32)
        used = lax.rem(iota((SLOTS, 1), 0), PAD) < CAP
        pick = onehot(jnp.where(used, index, -1) == iota((SLOTS, rows_here), 1))
        summed[...] += dot(high, pick, 1, 0) + dot(low, pick, 1, 0)

    tail = summed[body:width]
    for j in range(1, LANES // TAIL):
        tail = tail + summed[body + TAIL * j : body + TAIL * j + TAIL]
    total = jnp.concatenate([summed[0:body], tail], axis=0)
    new_sum = adagrad[...] + jnp.sum(total * total, axis=0, keepdims=True) * (1.0 / width)
    sum_out[...] = new_sum
    table_out[...] = table[...] - total * (LEARNING_RATE / jnp.sqrt(new_sum))

    part = ask_send.at[pl.ds(1, 7)]
    pltpu.make_async_copy(part, part, send_sems.at[0]).wait()
    part = asked.at[pl.ds(1, 15)]
    pltpu.make_async_copy(part, part, send_sems.at[3]).wait()
    for n, buffer in ((1, row_send), (2, grad_send)):
        part = buffer.at[pl.ds(1, DEVICES - 1)]
        pltpu.make_async_copy(part, part, send_sems.at[n]).wait()
    for dy in range(4):
        forward_copy(dy).wait_send()
        sibling_copy(dy).wait_send()
        if dy > 0:
            query_copy(dy).wait_send()
            home_copy(dy).wait_send()


def on_device(entity_table, adagrad_sum, relations, owner_map, head_ids, rel_ids, tail_ids, neg_ids):
    rows_here, width = entity_table.shape
    edges = head_ids.shape[0]
    neg_count = neg_ids.shape[0]
    count = 2 * edges + neg_count
    map_rows = owner_map.shape[0] // 128
    vmem = pl.BlockSpec(memory_space=pltpu.VMEM)
    hbm = pl.BlockSpec(memory_space=pl.ANY)
    wide = 4 * LANES
    slots = pltpu.VMEM((DEVICES, LINES, LANES), F32)
    parts = pltpu.VMEM((4, width, LANES), F32)
    sem = pltpu.SemaphoreType.DMA
    new_table, new_sum = pl.pallas_call(
        step_kernel,
        out_shape=(
            jax.ShapeDtypeStruct((width, rows_here), F32),
            jax.ShapeDtypeStruct((1, rows_here), F32),
        ),
        in_specs=[vmem, vmem, vmem, vmem, hbm, hbm, hbm, vmem],
        out_specs=(vmem, vmem),
        scratch_shapes=[
            pltpu.VMEM((map_rows, 128), jnp.int32),
            pltpu.VMEM((width, rows_here), F32),
            pltpu.VMEM((width, -(-relations.shape[0] // (REL * REL_PARTS)) * REL), F32),
            pltpu.VMEM((map_rows, 384), BF16),
            pltpu.VMEM((wide, rows_here), BF16),
            pltpu.VMEM((wide, rows_here), BF16),
            pltpu.VMEM((8, 128), jnp.int32),
            pltpu.VMEM((count, 1), F32),
            pltpu.VMEM((count, 1), F32),
            pltpu.VMEM((count, 1), F32),
            pltpu.VMEM((count, 1), F32),
            pltpu.VMEM((8, 128), F32),
            pltpu.VMEM((8, 16, 1, LANES), F32),
            pltpu.VMEM((8, 16, 1, LANES), F32),
            pltpu.VMEM((16, 1, LANES), F32),
            pltpu.VMEM((16, 1, LANES), F32),
            pltpu.VMEM((DEVICES * PAD, 1), F32),
            slots,
            slots,
            pltpu.VMEM((count, wide), F32),
            pltpu.VMEM((width, edges), F32),
            pltpu.VMEM((edges, wide), F32),
            pltpu.VMEM((2, neg_count, wide), BF16),
            pltpu.VMEM((neg_count, wide), F32),
            pltpu.VMEM((1, neg_count), F32),
            pltpu.VMEM((4, 2, width, LANES), F32),
            parts,
            parts,
            parts,
            parts,
            parts,
            pltpu.VMEM((2, count, wide), BF16),
            slots,
            slots,
            pltpu.VMEM((wide, rows_here), F32),
            sem((3,)),
            sem((2,)),
            sem((CHUNKS,)),
            sem((CHUNKS,)),
            sem((4, 2)),
            sem((4, 2)),
            sem((4,)),
            sem((4, 2)),
            sem((4, 2)),
        ],
        compiler_params=pltpu.CompilerParams(
            collective_id=0, has_side_effects=True, vmem_limit_bytes=LIMIT
        ),
    )(
        head_ids.reshape(1, edges),
        tail_ids.reshape(1, edges),
        neg_ids.reshape(neg_count // 128, 128),
        rel_ids.reshape(1, edges),
        owner_map.reshape(map_rows, 128),
        entity_table.T,
        relations.T,
        adagrad_sum.reshape(1, rows_here),
    )
    return new_table.T, new_sum.reshape(rows_here)


def solution(mesh):
    assert dict(mesh.shape) == {"dp": 16, "blk": 8}
    return jax.shard_map(
        on_device,
        mesh=mesh,
        in_specs=(
            P(("dp", "blk"), None),
            P(("dp", "blk")),
            P(),
            P(),
            P(("dp", "blk")),
            P(("dp", "blk")),
            P(("dp", "blk")),
            P(("dp", "blk")),
        ),
        out_specs=(P(("dp", "blk"), None), P(("dp", "blk"))),
        check_vma=False,
    )
```

```python
import functools

import jax
import jax.numpy as jnp
from jax import lax
from jax.experimental import pallas as pl
from jax.experimental.pallas import tpu as pltpu
from jax.sharding import PartitionSpec as P

MARGIN = 10.0
EPSILON = 1e-05
LEARNING_RATE = 0.1
MESH = pl.DeviceIdType.MESH
F32 = jnp.float32
BF16 = jnp.bfloat16
DEVICES = 128
CAP = 12
PAD = 16
GROUP = 16
CHUNKS = DEVICES // GROUP
SLOTS = GROUP * PAD
LINES = 40
LIMIT = 48 * 1024 * 1024
LANES = 128
TAIL = 16
REL = 256
REL_PARTS = 3


def split(x):
    high = x.astype(BF16)
    return high, (x - high.astype(F32)).astype(BF16)


def dot(a, b, ca, cb):
    return lax.dot_general(a, b, (((ca,), (cb,)), ((), ())), preferred_element_type=F32)


def dot3(a, b, ca, cb):
    return dot(a[0], b[0], ca, cb) + (dot(a[0], b[1], ca, cb) + dot(a[1], b[0], ca, cb))


def iota(shape, axis):
    return lax.broadcasted_iota(jnp.int32, shape, axis)


def onehot(mask):
    return jnp.where(mask, 1.0, 0.0).astype(BF16)


def to_column(row):
    n = row.shape[1]
    return jnp.sum(jnp.where(iota((n, n), 0) == iota((n, n), 1), row, 0.0), axis=1, keepdims=True)


def to_row(column):
    n = column.shape[0]
    return jnp.sum(jnp.where(iota((n, n), 0) == iota((n, n), 1), column, 0.0), axis=0, keepdims=True)


def tail_mask():
    return iota((GROUP, 8, LANES), 1) == iota((GROUP, 8, LANES), 2) // TAIL


def pack(buffer, c, full):
    full = full.reshape(GROUP, PAD, 4 * LANES)
    up, low = full[:, 0:8], full[:, 8:16]
    sub = iota((GROUP, 8, LANES), 1)
    first = sub < 4
    tail_up = jnp.sum(jnp.where(tail_mask(), up[:, :, 3 * LANES :], 0.0), axis=1, keepdims=True)
    tail_low = jnp.sum(
        jnp.where(tail_mask() & first, low[:, :, 3 * LANES :], 0.0), axis=1, keepdims=True
    )
    here = pl.ds(c * GROUP, GROUP)
    for n in range(3):
        buffer[here, 8 * n : 8 * n + 8, :] = up[:, :, LANES * n : LANES * n + LANES]
    buffer[here, 24:32, :] = jnp.where(first, low[:, :, 0:LANES], low[:, :, LANES : 2 * LANES])
    rest = jnp.where(sub == 4, tail_up, jnp.where(sub == 5, tail_low, 0.0))
    buffer[here, 32:40, :] = jnp.where(first, low[:, :, 2 * LANES : 3 * LANES], rest)


def unpack(buffer, c):
    part = buffer[pl.ds(c * GROUP, GROUP)]
    lines = [part[:, 8 * n : 8 * n + 8] for n in range(5)]
    first = iota((GROUP, 8, LANES), 1) < 4
    tail_up = jnp.where(tail_mask(), lines[4][:, 4:5], 0.0)
    tail_low = jnp.where(tail_mask() & first, lines[4][:, 5:6], 0.0)
    turned = pltpu.roll(lines[3].reshape(GROUP * 8, LANES), GROUP * 8 - 4, 0)
    turned = turned.reshape(GROUP, 8, LANES)
    up = jnp.concatenate([lines[0], lines[1], lines[2], tail_up], axis=2)
    low = jnp.concatenate([lines[3], turned, lines[4], tail_low], axis=2)
    return jnp.concatenate([up, low], axis=1).reshape(SLOTS, 4 * LANES)


def to_lines(x):
    tail = x[:, 3 * LANES :]
    for shift in (TAIL, 2 * TAIL, 4 * TAIL):
        tail = tail + pltpu.roll(tail, shift, 1)
    tail = tail.reshape(GROUP, 8, LANES)
    tail = jnp.sum(jnp.where(tail_mask(), tail, 0.0), axis=1)
    return jnp.concatenate([x[:, LANES * n : LANES * n + LANES] for n in range(3)] + [tail], axis=0)


def from_lines(lines):
    tail = lines[3 * LANES :].reshape(GROUP, 1, LANES)
    tail = jnp.where(tail_mask(), tail, 0.0).reshape(LANES, LANES)
    for shift in (4 * TAIL, 2 * TAIL, TAIL):
        tail = tail + pltpu.roll(tail, shift, 1)
    tail = jnp.where(iota((LANES, LANES), 1) < TAIL, tail, 0.0)
    return jnp.concatenate([lines[LANES * n : LANES * n + LANES] for n in range(3)] + [tail], axis=1)


def step_kernel(
    heads_hbm,
    tails_hbm,
    negs_hbm,
    rels_hbm,
    map_hbm,
    table_hbm,
    relations_hbm,
    adagrad_hbm,
    table_out,
    sum_out,
    heads,
    tails,
    negs,
    rels,
    adagrad,
    map_ref,
    table,
    relations,
    map_parts,
    table_high,
    table_low,
    ids,
    key_col,
    ask_col,
    local_col,
    slot_col,
    slot_row,
    ask_send,
    ask_mid,
    ask_sum,
    asked,
    index_col,
    row_send,
    rows,
    wanted,
    rel_acc,
    rel_rows,
    neg_pieces,
    block_acc,
    coef_cols,
    all_queries,
    parts,
    part_sibling,
    part_sum,
    part_recv,
    grad_pieces,
    grad_send,
    grads,
    summed,
    load_sem,
    ask_sems,
    row_sems,
    grad_sems,
    half_sems,
    query_sems,
    part_sems,
    send_sems,
    half_send_sems,
    query_send_sems,
    part_send_sems,
):
    dp = lax.axis_index("dp")
    blk = lax.axis_index("blk")
    mx, mz = dp // 4, lax.rem(dp, 4)
    my, mc = blk // 2, lax.rem(blk, 2)
    width = table.shape[0]
    body = 3 * LANES
    rows_here = table.shape[1]
    edges = heads.shape[1]
    rel_chunks = relations_hbm.shape[1] // REL
    rel_step = relations.shape[1] // REL
    rel_cuts = [min(n * rel_step, rel_chunks) for n in range(REL_PARTS + 1)]

    def deltas(i):
        a, b, c, dc = lax.rem(i, 4), lax.rem(i // 4, 4), lax.rem(i // 16, 4), i // 64
        return a, lax.rem(a + b, 4), lax.rem(a + c, 4), dc

    def ahead(i):
        dx, dy, dz, dc = deltas(i)
        return (
            lax.rem(mx + dx, 4) * 4 + lax.rem(mz + dz, 4),
            lax.rem(my + dy, 4) * 2 + lax.rem(mc + dc, 2),
        )

    def behind(i):
        dx, dy, dz, dc = deltas(i)
        return (
            lax.rem(mx + 4 - dx, 4) * 4 + lax.rem(mz + 4 - dz, 4),
            lax.rem(my + 4 - dy, 4) * 2 + lax.rem(mc + dc, 2),
        )

    def remote(src, dst, send, recv, device):
        return pltpu.make_async_remote_copy(
            src_ref=src,
            dst_ref=dst,
            send_sem=send,
            recv_sem=recv,
            device_id=device,
            device_id_type=MESH,
        )

    load_map = pltpu.make_async_copy(map_hbm, map_ref, load_sem.at[0])
    load_table = pltpu.make_async_copy(table_hbm, table, load_sem.at[1])

    def load_relations(half):
        first, lanes = rel_cuts[half] * REL, (rel_cuts[half + 1] - rel_cuts[half]) * REL
        part = relations_hbm.at[:, pl.ds(first, lanes)]
        return pltpu.make_async_copy(part, relations.at[:, pl.ds(0, lanes)], load_sem.at[2])

    small = [
        pltpu.make_async_copy(src, dst, load_sem.at[3 + n])
        for n, (src, dst) in enumerate(
            [
                (heads_hbm, heads),
                (tails_hbm, tails),
                (negs_hbm, negs),
                (rels_hbm, rels),
                (adagrad_hbm, adagrad),
            ]
        )
    ]
    for copy in small:
        copy.start()
    load_map.start()
    load_table.start()
    load_relations(0).start()
    barrier = pltpu.get_barrier_semaphore()

    def in_group(r):
        return dp, lax.rem(my + lax.rem(r, 4), 4) * 2 + lax.rem(mc + r // 4, 2)

    def in_plane(p):
        return lax.rem(mx + p // 4, 4) * 4 + lax.rem(mz + lax.rem(p, 4), 4), blk

    @pl.loop(1, 8)
    def _(r):
        pl.semaphore_signal(barrier, inc=1, device_id=in_group(r), device_id_type=MESH)

    @pl.loop(1, 16)
    def _(p):
        pl.semaphore_signal(barrier, inc=1, device_id=in_plane(p), device_id_type=MESH)

    for copy in small:
        copy.wait()
    ids[0:1, :] = heads[...]
    ids[1:2, :] = tails[...]
    ids[2:6, :] = negs[...]
    load_map.wait()
    position_of = map_ref[...]
    map_parts[:, 0:128] = (position_of & 255).astype(F32).astype(BF16)
    map_parts[:, 128:256] = ((position_of >> 8) & 255).astype(F32).astype(BF16)
    map_parts[:, 256:384] = (position_of >> 16).astype(F32).astype(BF16)

    @pl.loop(0, 6)
    def _(t):
        column = to_column(ids[pl.ds(t, 1), :].astype(F32)).astype(jnp.int32)
        line = onehot((column >> 7) == iota((128, map_ref.shape[0]), 1))
        found = dot(line, map_parts[...], 1, 0)
        lane = (column & 127) == iota((128, 128), 1)
        piece = [
            jnp.sum(jnp.where(lane, found[:, 128 * p : 128 * p + 128], 0.0), axis=1, keepdims=True)
            for p in range(3)
        ]
        position = (piece[0] + 256.0 * piece[1] + 65536.0 * piece[2]).astype(jnp.int32)
        owner = position >> 11
        dx = ((owner >> 5) - mx) & 3
        dz = ((owner >> 3) - mz) & 3
        dy = ((owner >> 1) - my) & 3
        dc = (owner - mc) & 1
        key = dc * 64 + ((dz - dx) & 3) * 16 + ((dy - dx) & 3) * 4 + dx
        ask = (dc * 4 + dy) * 16 + dx * 4 + dz
        where = pl.ds(pl.multiple_of(t * 128, 128), 128)
        key_col[where, :] = key.astype(F32)
        ask_col[where, :] = ask.astype(F32)
        local_col[where, :] = (position & (rows_here - 1)).astype(F32)

    count = key_col.shape[0]
    keys = key_col[...]
    key_hot = onehot(ask_col[...].astype(jnp.int32) == iota((count, DEVICES), 1))
    earlier = onehot(iota((count, count), 1) < iota((count, count), 0))
    before = dot(earlier, key_hot, 1, 0)
    rank = jnp.sum(before * key_hot.astype(F32), axis=1, keepdims=True)
    local = local_col[...].astype(jnp.int32)
    place = rank.astype(jnp.int32)
    lane = iota((count, LANES), 1)
    spread = lane - (ask_col[...].astype(jnp.int32) // 16) * PAD
    spot = (place == spread) | ((place >= 8) & (place + 4 == spread))
    upper = jnp.where(spot, (local >> 8).astype(F32), 0.0).astype(BF16)
    lower = jnp.where(spot, (local & 255).astype(F32), 0.0).astype(BF16)
    asks = 256.0 * dot(key_hot, upper, 0, 0) + dot(key_hot, lower, 0, 0)
    ask_send[...] = asks.reshape(8, 16, 1, LANES)
    slot = keys * float(PAD) + rank
    slot_col[...] = slot
    for t in range(6):
        slot_row[t : t + 1, :] = to_row(slot[128 * t : 128 * t + 128])

    load_table.wait()
    high, low = split(table[...])
    table_high[0:width] = high
    table_low[0:width] = low
    for j in range(1, LANES // TAIL):
        table_high[body + TAIL * j : body + TAIL * j + TAIL] = high[body:]
        table_low[body + TAIL * j : body + TAIL * j + TAIL] = low[body:]
    summed[...] = jnp.zeros_like(summed)
    wanted[...] = jnp.zeros_like(wanted)
    ask_mid[0] = ask_send[0]

    pl.semaphore_wait(barrier, 22)

    def group_ask(r):
        return remote(ask_send.at[r], ask_mid.at[r], send_sems.at[0], ask_sems.at[0], in_group(r))

    def plane_ask(p):
        return remote(ask_sum.at[p], asked.at[p], send_sems.at[3], ask_sems.at[1], in_plane(p))

    @pl.loop(1, 8)
    def _(r):
        group_ask(r).start()

    part = ask_mid.at[pl.ds(1, 7)]
    pltpu.make_async_copy(part, part, ask_sems.at[0]).wait()
    ask_sum[...] = jnp.sum(ask_mid[...], axis=0)

    @pl.loop(1, 16)
    def _(p):
        plane_ask(p).start()

    asked[0] = ask_sum[0]
    part = asked.at[pl.ds(1, 15)]
    pltpu.make_async_copy(part, part, ask_sems.at[1]).wait()

    def wait_chunk(buffer, sems, c):
        @pl.when(c == 0)
        def _():
            part = buffer.at[pl.ds(1, GROUP - 1)]
            pltpu.make_async_copy(part, part, sems.at[0]).wait()

        @pl.when(c > 0)
        def _():
            part = buffer.at[pl.ds(c * GROUP, GROUP)]
            pltpu.make_async_copy(part, part, sems.at[c]).wait()

    def row_copy(i):
        return remote(
            row_send.at[i],
            rows.at[i],
            send_sems.at[1],
            row_sems.at[i // GROUP],
            behind(i),
        )

    @pl.loop(0, CHUNKS)
    def _(c):
        parts = []
        for g in range(GROUP):
            dx, dy, dz, dc = deltas(c * GROUP + g)
            line = jnp.broadcast_to(asked[dx * 4 + dz], (PAD, LANES))
            lane = iota((PAD, LANES), 1) - (dc * 4 + dy) * PAD
            parts.append(jnp.where(lane == iota((PAD, LANES), 0), line, 0.0))
        index = jnp.sum(jnp.concatenate(parts, axis=0), axis=1, keepdims=True)
        index_col[pl.ds(pl.multiple_of(c * SLOTS, SLOTS), SLOTS), :] = index
        pick = onehot(index.astype(jnp.int32) == iota((SLOTS, rows_here), 1))
        picked = dot(pick, table_high[...], 1, 1) + dot(pick, table_low[...], 1, 1)
        pack(row_send, c, picked)

        @pl.when(c == 0)
        def _():
            rows[0] = row_send[0]

        @pl.loop(0, GROUP)
        def _(g):
            @pl.when(c * GROUP + g > 0)
            def _():
                row_copy(c * GROUP + g).start()

    rel_acc[...] = jnp.zeros_like(rel_acc)
    for half in range(REL_PARTS):
        load_relations(half).wait()

        @pl.loop(0, rel_cuts[half + 1] - rel_cuts[half])
        def _(t):
            high, low = split(relations[:, pl.ds(pl.multiple_of(t * REL, REL), REL)])
            base = (t + rel_cuts[half]) * REL
            pick = onehot(iota((REL, edges), 0) + base == rels[...])
            found = dot(jnp.concatenate([high, low], axis=0), pick, 1, 0)
            rel_acc[...] += found[0:width] + found[width:]

        if half + 1 < REL_PARTS:
            load_relations(half + 1).start()

    rel_rows[...] = jnp.zeros_like(rel_rows)
    rel_rows[:, 0:width] = rel_acc[...].T

    @pl.loop(0, CHUNKS)
    def _(c):
        wait_chunk(rows, row_sems, c)
        high, low = split(unpack(rows, c))
        place = onehot(slot_col[...].astype(jnp.int32) - c * SLOTS == iota((count, SLOTS), 1))
        wanted[...] += dot(place, high, 1, 0) + dot(place, low, 1, 0)

    high, low = split(wanted[:, body:])
    fold = onehot(lax.rem(iota((LANES, LANES), 0), TAIL) == iota((LANES, LANES), 1))
    wanted[:, body:] = dot(high, fold, 1, 0) + dot(low, fold, 1, 0)
    queries = wanted[0:edges, :] + rel_rows[...]
    residue = queries - wanted[edges : 2 * edges, :]
    pos_dist = jnp.sqrt(jnp.sum(residue * residue, axis=1, keepdims=True) + EPSILON)
    grad_pos = (1.0 / (1.0 + jnp.exp(MARGIN - pos_dist)) / pos_dist) * residue
    all_queries[0, 0] = to_lines(queries)

    sibling = (dp, blk + 1 - 2 * mc)

    def at_y(dy):
        return dp, lax.rem(my + dy, 4) * 2 + mc

    def half_copy(dy, half):
        lines = pl.ds(half * (width // 2), width // 2)
        return remote(
            all_queries.at[0, 0, lines, :],
            all_queries.at[dy, 0, lines, :],
            half_send_sems.at[dy, half],
            half_sems.at[dy, half],
            at_y(dy),
        )

    def relay_copy(half):
        lines = pl.ds(half * (width // 2), width // 2)
        return remote(
            all_queries.at[1 + 2 * half, 0, lines, :],
            all_queries.at[2, 0, lines, :],
            half_send_sems.at[2, half],
            half_sems.at[2, half],
            at_y(1 + 2 * half),
        )

    def forward_copy(dy):
        return remote(
            all_queries.at[dy, 0],
            all_queries.at[dy, 1],
            query_send_sems.at[dy],
            query_sems.at[dy],
            sibling,
        )

    for dy, half in ((1, 0), (3, 1), (1, 1), (3, 0)):
        half_copy(dy, half).start()
    forward_copy(0).start()
    negatives = wanted[2 * edges :, :]
    high, low = split(negatives)
    neg_pieces[0] = high
    neg_pieces[1] = low
    neg_col = jnp.sum(negatives * negatives, axis=1, keepdims=True)
    neg_count = negatives.shape[0]
    neg_sq = jnp.concatenate(
        [to_row(neg_col[128 * t : 128 * t + 128]) for t in range(neg_count // 128)], axis=1
    )
    block_acc[...] = jnp.zeros_like(block_acc)
    coef_cols[...] = jnp.zeros_like(coef_cols)
    weight = 8.0 * neg_count

    def sibling_copy(dy):
        return remote(
            parts.at[dy, 1],
            part_sibling.at[dy],
            part_send_sems.at[dy, 0],
            part_sems.at[dy, 0],
            sibling,
        )

    def home_copy(dy):
        return remote(
            part_sum.at[dy],
            part_recv.at[dy],
            part_send_sems.at[dy, 1],
            part_sems.at[dy, 1],
            (dp, lax.rem(my + 4 - dy, 4) * 2 + mc),
        )

    def block_terms(block):
        pieces = split(block)
        block_sq = jnp.sum(block * block, axis=1, keepdims=True)
        neg_parts = (neg_pieces[0], neg_pieces[1])
        inner = dot3(pieces, neg_parts, 1, 1)
        dist = jnp.sqrt(block_sq + neg_sq - 2.0 * inner + EPSILON)
        coef = -1.0 / ((1.0 + jnp.exp(dist - MARGIN)) * (weight * dist))
        coef_parts = split(coef)
        coef_cols[...] += jnp.sum(coef, axis=0, keepdims=True)
        block_acc[...] += dot3(coef_parts, pieces, 0, 0)
        return block * jnp.sum(coef, axis=1, keepdims=True) - dot3(coef_parts, neg_parts, 1, 0)

    def finish(dy):
        sibling_copy(dy).wait_recv()
        part_sum[dy] = parts[dy, 0] + part_sibling[dy]

    @pl.loop(0, 8)
    def _(u):
        v, w = u // 2, lax.rem(u, 2)
        far = (v + 1) // 2
        dy = far + lax.rem(far, 2) * 2 * w
        dc = v // 2 + (1 - (lax.rem(v, 3) + 1) // 2) * w * (1 - 2 * (v // 2))

        @pl.when(u == 2)
        def _():
            half_copy(1, 0).wait_recv()
            relay_copy(0).start()
            half_copy(3, 1).wait_recv()
            relay_copy(1).start()
            half_copy(1, 1).wait_recv()
            forward_copy(1).start()
            half_copy(3, 0).wait_recv()
            forward_copy(3).start()

        @pl.when(u == 4)
        def _():
            relay_copy(0).wait_recv()
            relay_copy(1).wait_recv()
            forward_copy(2).start()

        @pl.when(dc == 1)
        def _():
            forward_copy(dy).wait_recv()

        parts[dy, dc] = to_lines(block_terms(from_lines(all_queries[dy, dc])))

        @pl.when(dc == 1)
        def _():
            sibling_copy(dy).start()

        @pl.when((u == 5) | (u == 6))
        def _():
            last = 1 + 2 * (u - 5)
            finish(last)
            home_copy(last).start()

    finish(2)
    home_copy(2).start()
    finish(0)
    for dy in (1, 3, 2):
        home_copy(dy).wait_recv()
    grad_neg = from_lines((part_sum[0] + part_recv[1]) + (part_recv[2] + part_recv[3]))
    high, low = split(grad_pos + grad_neg)
    grad_pieces[0, 0:edges] = high
    grad_pieces[1, 0:edges] = low
    high, low = split(-grad_pos)
    grad_pieces[0, edges : 2 * edges] = high
    grad_pieces[1, edges : 2 * edges] = low
    coef_col = jnp.concatenate(
        [to_column(coef_cols[:, 128 * t : 128 * t + 128]) for t in range(neg_count // 128)], axis=0
    )
    high, low = split(wanted[2 * edges :, :] * coef_col - block_acc[...])
    grad_pieces[0, 2 * edges :] = high
    grad_pieces[1, 2 * edges :] = low

    spread = onehot(iota((LANES, LANES), 0) == lax.rem(iota((LANES, LANES), 1), TAIL))
    for n in range(2):
        grad_pieces[n, :, body:] = dot(grad_pieces[n, :, body:], spread, 1, 0).astype(BF16)

    def grad_copy(i):
        return remote(
            grad_send.at[i],
            grads.at[i],
            send_sems.at[2],
            grad_sems.at[i // GROUP],
            ahead(i),
        )

    @pl.loop(0, CHUNKS)
    def _(c):
        line = iota((SLOTS, LANES), 0)
        base = line + c * SLOTS - jnp.where(lax.rem(line, PAD) < CAP, 0, PAD - CAP)
        place = jnp.concatenate(
            [onehot(slot_row[t : t + 1, :].astype(jnp.int32) == base) for t in range(6)], axis=1
        )
        packed = dot(place, grad_pieces[0], 1, 0) + dot(place, grad_pieces[1], 1, 0)
        pack(grad_send, c, packed)

        @pl.when(c == 0)
        def _():
            grads[0] = grad_send[0]

        @pl.loop(0, GROUP)
        def _(g):
            @pl.when(c * GROUP + g > 0)
            def _():
                grad_copy(c * GROUP + g).start()

    @pl.loop(0, CHUNKS)
    def _(c):
        wait_chunk(grads, grad_sems, c)
        high, low = split(unpack(grads, c).T)
        index = index_col[pl.ds(pl.multiple_of(c * SLOTS, SLOTS), SLOTS), :].astype(jnp.int32)
        used = lax.rem(iota((SLOTS, 1), 0), PAD) < CAP
        pick = onehot(jnp.where(used, index, -1) == iota((SLOTS, rows_here), 1))
        summed[...] += dot(high, pick, 1, 0) + dot(low, pick, 1, 0)

    tail = summed[body:width]
    for j in range(1, LANES // TAIL):
        tail = tail + summed[body + TAIL * j : body + TAIL * j + TAIL]
    total = jnp.concatenate([summed[0:body], tail], axis=0)
    new_sum = adagrad[...] + jnp.sum(total * total, axis=0, keepdims=True) * (1.0 / width)
    sum_out[...] = new_sum
    table_out[...] = table[...] - total * (LEARNING_RATE / jnp.sqrt(new_sum))

    part = ask_send.at[pl.ds(1, 7)]
    pltpu.make_async_copy(part, part, send_sems.at[0]).wait()
    part = asked.at[pl.ds(1, 15)]
    pltpu.make_async_copy(part, part, send_sems.at[3]).wait()
    for n, buffer in ((1, row_send), (2, grad_send)):
        part = buffer.at[pl.ds(1, DEVICES - 1)]
        pltpu.make_async_copy(part, part, send_sems.at[n]).wait()
    for dy in range(4):
        forward_copy(dy).wait_send()
        sibling_copy(dy).wait_send()
        if dy > 0:
            home_copy(dy).wait_send()
    for half in range(2):
        half_copy(1, half).wait_send()
        half_copy(3, half).wait_send()
        relay_copy(half).wait_send()


def on_device(entity_table, adagrad_sum, relations, owner_map, head_ids, rel_ids, tail_ids, neg_ids):
    rows_here, width = entity_table.shape
    edges = head_ids.shape[0]
    neg_count = neg_ids.shape[0]
    count = 2 * edges + neg_count
    map_rows = owner_map.shape[0] // 128
    vmem = pl.BlockSpec(memory_space=pltpu.VMEM)
    hbm = pl.BlockSpec(memory_space=pltpu.HBM)
    wide = 4 * LANES
    slots = pltpu.VMEM((DEVICES, LINES, LANES), F32)
    parts = pltpu.VMEM((4, width, LANES), F32)
    sem = pltpu.SemaphoreType.DMA
    new_table, new_sum = pl.pallas_call(
        step_kernel,
        out_shape=(
            jax.ShapeDtypeStruct((width, rows_here), F32),
            jax.ShapeDtypeStruct((1, rows_here), F32),
        ),
        in_specs=[hbm] * 8,
        out_specs=(vmem, vmem),
        scratch_shapes=[
            pltpu.VMEM((1, edges), jnp.int32),
            pltpu.VMEM((1, edges), jnp.int32),
            pltpu.VMEM((neg_count // LANES, LANES), jnp.int32),
            pltpu.VMEM((1, edges), jnp.int32),
            pltpu.VMEM((1, rows_here), F32),
            pltpu.VMEM((map_rows, 128), jnp.int32),
            pltpu.VMEM((width, rows_here), F32),
            pltpu.VMEM((width, -(-relations.shape[0] // (REL * REL_PARTS)) * REL), F32),
            pltpu.VMEM((map_rows, 384), BF16),
            pltpu.VMEM((wide, rows_here), BF16),
            pltpu.VMEM((wide, rows_here), BF16),
            pltpu.VMEM((8, 128), jnp.int32),
            pltpu.VMEM((count, 1), F32),
            pltpu.VMEM((count, 1), F32),
            pltpu.VMEM((count, 1), F32),
            pltpu.VMEM((count, 1), F32),
            pltpu.VMEM((8, 128), F32),
            pltpu.VMEM((8, 16, 1, LANES), F32),
            pltpu.VMEM((8, 16, 1, LANES), F32),
            pltpu.VMEM((16, 1, LANES), F32),
            pltpu.VMEM((16, 1, LANES), F32),
            pltpu.VMEM((DEVICES * PAD, 1), F32),
            slots,
            slots,
            pltpu.VMEM((count, wide), F32),
            pltpu.VMEM((width, edges), F32),
            pltpu.VMEM((edges, wide), F32),
            pltpu.VMEM((2, neg_count, wide), BF16),
            pltpu.VMEM((neg_count, wide), F32),
            pltpu.VMEM((1, neg_count), F32),
            pltpu.VMEM((4, 2, width, LANES), F32),
            pltpu.VMEM((4, 2, width, LANES), F32),
            parts,
            parts,
            parts,
            pltpu.VMEM((2, count, wide), BF16),
            slots,
            slots,
            pltpu.VMEM((wide, rows_here), F32),
            sem((8,)),
            sem((2,)),
            sem((CHUNKS,)),
            sem((CHUNKS,)),
            sem((4, 2)),
            sem((4,)),
            sem((4, 2)),
            sem((4,)),
            sem((4, 2)),
            sem((4,)),
            sem((4, 2)),
        ],
        compiler_params=pltpu.CompilerParams(
            collective_id=0, has_side_effects=True, vmem_limit_bytes=LIMIT
        ),
    )(
        pltpu.with_memory_space_constraint(head_ids.reshape(1, edges), pltpu.HBM),
        pltpu.with_memory_space_constraint(tail_ids.reshape(1, edges), pltpu.HBM),
        pltpu.with_memory_space_constraint(neg_ids.reshape(neg_count // 128, 128), pltpu.HBM),
        pltpu.with_memory_space_constraint(rel_ids.reshape(1, edges), pltpu.HBM),
        pltpu.with_memory_space_constraint(owner_map.reshape(map_rows, 128), pltpu.HBM),
        pltpu.with_memory_space_constraint(entity_table.T, pltpu.HBM),
        pltpu.with_memory_space_constraint(relations.T, pltpu.HBM),
        pltpu.with_memory_space_constraint(adagrad_sum.reshape(1, rows_here), pltpu.HBM),
    )
    return new_table.T, new_sum.reshape(rows_here)


def solution(mesh):
    assert dict(mesh.shape) == {"dp": 16, "blk": 8}
    return jax.shard_map(
        on_device,
        mesh=mesh,
        in_specs=(
            P(("dp", "blk"), None),
            P(("dp", "blk")),
            P(),
            P(),
            P(("dp", "blk")),
            P(("dp", "blk")),
            P(("dp", "blk")),
            P(("dp", "blk")),
        ),
        out_specs=(P(("dp", "blk"), None), P(("dp", "blk"))),
        check_vma=False,
    )
```

```python
import functools

import jax
import jax.numpy as jnp
from jax import lax
from jax.experimental import pallas as pl
from jax.experimental.pallas import tpu as pltpu
from jax.sharding import PartitionSpec as P

MARGIN = 10.0
EPSILON = 1e-05
LEARNING_RATE = 0.1
MESH = pl.DeviceIdType.MESH
F32 = jnp.float32
BF16 = jnp.bfloat16
DEVICES = 128
CAP = 12
PAD = 16
GROUP = 16
CHUNKS = DEVICES // GROUP
SLOTS = GROUP * PAD
LINES = 40
LIMIT = 50 * 1024 * 1024
LANES = 128
TAIL = 16
REL = 256
REL_PARTS = 3


def split(x):
    high = x.astype(BF16)
    return high, (x - high.astype(F32)).astype(BF16)


def dot(a, b, ca, cb):
    return lax.dot_general(a, b, (((ca,), (cb,)), ((), ())), preferred_element_type=F32)


def dot3(a, b, ca, cb):
    return dot(a[0], b[0], ca, cb) + (dot(a[0], b[1], ca, cb) + dot(a[1], b[0], ca, cb))


def iota(shape, axis):
    return lax.broadcasted_iota(jnp.int32, shape, axis)


def onehot(mask):
    return jnp.where(mask, 1.0, 0.0).astype(BF16)


def to_column(row):
    n = row.shape[1]
    return jnp.sum(jnp.where(iota((n, n), 0) == iota((n, n), 1), row, 0.0), axis=1, keepdims=True)


def to_row(column):
    n = column.shape[0]
    return jnp.sum(jnp.where(iota((n, n), 0) == iota((n, n), 1), column, 0.0), axis=0, keepdims=True)


def tail_mask():
    return iota((GROUP, 8, LANES), 1) == iota((GROUP, 8, LANES), 2) // TAIL


def pack(buffer, c, full):
    full = full.reshape(GROUP, PAD, 4 * LANES)
    up, low = full[:, 0:8], full[:, 8:16]
    sub = iota((GROUP, 8, LANES), 1)
    first = sub < 4
    tail_up = jnp.sum(jnp.where(tail_mask(), up[:, :, 3 * LANES :], 0.0), axis=1, keepdims=True)
    tail_low = jnp.sum(
        jnp.where(tail_mask() & first, low[:, :, 3 * LANES :], 0.0), axis=1, keepdims=True
    )
    here = pl.ds(c * GROUP, GROUP)
    for n in range(3):
        buffer[here, 8 * n : 8 * n + 8, :] = up[:, :, LANES * n : LANES * n + LANES]
    buffer[here, 24:32, :] = jnp.where(first, low[:, :, 0:LANES], low[:, :, LANES : 2 * LANES])
    rest = jnp.where(sub == 4, tail_up, jnp.where(sub == 5, tail_low, 0.0))
    buffer[here, 32:40, :] = jnp.where(first, low[:, :, 2 * LANES : 3 * LANES], rest)


def unpack(buffer, c):
    part = buffer[pl.ds(c * GROUP, GROUP)]
    lines = [part[:, 8 * n : 8 * n + 8] for n in range(5)]
    first = iota((GROUP, 8, LANES), 1) < 4
    tail_up = jnp.where(tail_mask(), lines[4][:, 4:5], 0.0)
    tail_low = jnp.where(tail_mask() & first, lines[4][:, 5:6], 0.0)
    turned = pltpu.roll(lines[3].reshape(GROUP * 8, LANES), GROUP * 8 - 4, 0)
    turned = turned.reshape(GROUP, 8, LANES)
    up = jnp.concatenate([lines[0], lines[1], lines[2], tail_up], axis=2)
    low = jnp.concatenate([lines[3], turned, lines[4], tail_low], axis=2)
    return jnp.concatenate([up, low], axis=1).reshape(SLOTS, 4 * LANES)


def to_lines(x):
    tail = x[:, 3 * LANES :]
    for shift in (TAIL, 2 * TAIL, 4 * TAIL):
        tail = tail + pltpu.roll(tail, shift, 1)
    tail = tail.reshape(GROUP, 8, LANES)
    tail = jnp.sum(jnp.where(tail_mask(), tail, 0.0), axis=1)
    return jnp.concatenate([x[:, LANES * n : LANES * n + LANES] for n in range(3)] + [tail], axis=0)


def from_lines(lines):
    tail = lines[3 * LANES :].reshape(GROUP, 1, LANES)
    tail = jnp.where(tail_mask(), tail, 0.0).reshape(LANES, LANES)
    for shift in (4 * TAIL, 2 * TAIL, TAIL):
        tail = tail + pltpu.roll(tail, shift, 1)
    tail = jnp.where(iota((LANES, LANES), 1) < TAIL, tail, 0.0)
    return jnp.concatenate([lines[LANES * n : LANES * n + LANES] for n in range(3)] + [tail], axis=1)


def step_kernel(
    heads_hbm,
    tails_hbm,
    negs_hbm,
    rels_hbm,
    map_hbm,
    table_hbm,
    relations_hbm,
    adagrad_hbm,
    table_out,
    sum_out,
    heads,
    tails,
    negs,
    rels,
    adagrad,
    map_ref,
    table,
    relations,
    map_parts,
    table_high,
    table_low,
    ids,
    key_col,
    ask_col,
    local_col,
    slot_col,
    slot_row,
    ask_send,
    ask_mid,
    ask_sum,
    asked,
    index_col,
    row_send,
    rows,
    wanted,
    rel_acc,
    rel_rows,
    neg_pieces,
    block_acc,
    coef_cols,
    all_queries,
    parts,
    part_sibling,
    part_sum,
    part_recv,
    grad_pieces,
    grad_send,
    grads,
    summed,
    load_sem,
    ask_sems,
    row_sems,
    grad_sems,
    half_sems,
    query_sems,
    part_sems,
    send_sems,
    half_send_sems,
    query_send_sems,
    part_send_sems,
):
    dp = lax.axis_index("dp")
    blk = lax.axis_index("blk")
    mx, mz = dp // 4, lax.rem(dp, 4)
    my, mc = blk // 2, lax.rem(blk, 2)
    width = table.shape[0]
    body = 3 * LANES
    rows_here = table.shape[1]
    edges = heads.shape[1]
    rel_chunks = relations_hbm.shape[1] // REL
    rel_step = relations.shape[1] // REL
    rel_cuts = [min(n * rel_step, rel_chunks) for n in range(REL_PARTS + 1)]

    def deltas(i):
        a, b, c, dc = lax.rem(i, 4), lax.rem(i // 4, 4), lax.rem(i // 16, 4), i // 64
        return a, lax.rem(a + b, 4), lax.rem(a + c, 4), dc

    def ahead(i):
        dx, dy, dz, dc = deltas(i)
        return (
            lax.rem(mx + dx, 4) * 4 + lax.rem(mz + dz, 4),
            lax.rem(my + dy, 4) * 2 + lax.rem(mc + dc, 2),
        )

    def behind(i):
        dx, dy, dz, dc = deltas(i)
        return (
            lax.rem(mx + 4 - dx, 4) * 4 + lax.rem(mz + 4 - dz, 4),
            lax.rem(my + 4 - dy, 4) * 2 + lax.rem(mc + dc, 2),
        )

    def remote(src, dst, send, recv, device):
        return pltpu.make_async_remote_copy(
            src_ref=src,
            dst_ref=dst,
            send_sem=send,
            recv_sem=recv,
            device_id=device,
            device_id_type=MESH,
        )

    load_map = pltpu.make_async_copy(map_hbm, map_ref, load_sem.at[0])
    load_table = pltpu.make_async_copy(table_hbm, table, load_sem.at[1])

    def load_relations(half):
        first, lanes = rel_cuts[half] * REL, (rel_cuts[half + 1] - rel_cuts[half]) * REL
        part = relations_hbm.at[:, pl.ds(first, lanes)]
        return pltpu.make_async_copy(part, relations.at[:, pl.ds(0, lanes)], load_sem.at[2])

    small = [
        pltpu.make_async_copy(src, dst, load_sem.at[3 + n])
        for n, (src, dst) in enumerate(
            [
                (heads_hbm, heads),
                (tails_hbm, tails),
                (negs_hbm, negs),
                (rels_hbm, rels),
                (adagrad_hbm, adagrad),
            ]
        )
    ]
    for copy in small:
        copy.start()
    load_map.start()
    load_table.start()
    load_relations(0).start()
    barrier = pltpu.get_barrier_semaphore()

    def in_group(r):
        return dp, lax.rem(my + lax.rem(r, 4), 4) * 2 + lax.rem(mc + r // 4, 2)

    def in_plane(p):
        return lax.rem(mx + p // 4, 4) * 4 + lax.rem(mz + lax.rem(p, 4), 4), blk

    @pl.loop(1, 8)
    def _(r):
        pl.semaphore_signal(barrier, inc=1, device_id=in_group(r), device_id_type=MESH)

    @pl.loop(1, 16)
    def _(p):
        pl.semaphore_signal(barrier, inc=1, device_id=in_plane(p), device_id_type=MESH)

    for copy in small:
        copy.wait()
    ids[0:1, :] = heads[...]
    ids[1:2, :] = tails[...]
    ids[2:6, :] = negs[...]
    load_map.wait()
    position_of = map_ref[...]
    map_parts[:, 0:128] = (position_of & 255).astype(F32).astype(BF16)
    map_parts[:, 128:256] = ((position_of >> 8) & 255).astype(F32).astype(BF16)
    map_parts[:, 256:384] = (position_of >> 16).astype(F32).astype(BF16)

    @pl.loop(0, 6)
    def _(t):
        column = to_column(ids[pl.ds(t, 1), :].astype(F32)).astype(jnp.int32)
        line = onehot((column >> 7) == iota((128, map_ref.shape[0]), 1))
        found = dot(line, map_parts[...], 1, 0)
        lane = (column & 127) == iota((128, 128), 1)
        piece = [
            jnp.sum(jnp.where(lane, found[:, 128 * p : 128 * p + 128], 0.0), axis=1, keepdims=True)
            for p in range(3)
        ]
        position = (piece[0] + 256.0 * piece[1] + 65536.0 * piece[2]).astype(jnp.int32)
        owner = position >> 11
        dx = ((owner >> 5) - mx) & 3
        dz = ((owner >> 3) - mz) & 3
        dy = ((owner >> 1) - my) & 3
        dc = (owner - mc) & 1
        key = dc * 64 + ((dz - dx) & 3) * 16 + ((dy - dx) & 3) * 4 + dx
        ask = (dc * 4 + dy) * 16 + dx * 4 + dz
        where = pl.ds(pl.multiple_of(t * 128, 128), 128)
        key_col[where, :] = key.astype(F32)
        ask_col[where, :] = ask.astype(F32)
        local_col[where, :] = (position & (rows_here - 1)).astype(F32)

    count = key_col.shape[0]
    keys = key_col[...]
    key_hot = onehot(ask_col[...].astype(jnp.int32) == iota((count, DEVICES), 1))
    earlier = onehot(iota((count, count), 1) < iota((count, count), 0))
    before = dot(earlier, key_hot, 1, 0)
    rank = jnp.sum(before * key_hot.astype(F32), axis=1, keepdims=True)
    local = local_col[...].astype(jnp.int32)
    place = rank.astype(jnp.int32)
    lane = iota((count, LANES), 1)
    spread = lane - (ask_col[...].astype(jnp.int32) // 16) * PAD
    spot = (place == spread) | ((place >= 8) & (place + 4 == spread))
    upper = jnp.where(spot, (local >> 8).astype(F32), 0.0).astype(BF16)
    lower = jnp.where(spot, (local & 255).astype(F32), 0.0).astype(BF16)
    asks = 256.0 * dot(key_hot, upper, 0, 0) + dot(key_hot, lower, 0, 0)
    ask_send[...] = asks.reshape(8, 16, 1, LANES)
    slot = keys * float(PAD) + rank
    slot_col[...] = slot
    for t in range(6):
        slot_row[t : t + 1, :] = to_row(slot[128 * t : 128 * t + 128])

    load_table.wait()
    high, low = split(table[...])
    table_high[0:width] = high
    table_low[0:width] = low
    for j in range(1, LANES // TAIL):
        table_high[body + TAIL * j : body + TAIL * j + TAIL] = high[body:]
        table_low[body + TAIL * j : body + TAIL * j + TAIL] = low[body:]
    summed[...] = jnp.zeros_like(summed)
    wanted[...] = jnp.zeros_like(wanted)
    ask_mid[0] = ask_send[0]

    pl.semaphore_wait(barrier, 22)

    def group_ask(r):
        return remote(ask_send.at[r], ask_mid.at[r], send_sems.at[0], ask_sems.at[0], in_group(r))

    def plane_ask(p):
        return remote(ask_sum.at[p], asked.at[p], send_sems.at[3], ask_sems.at[1], in_plane(p))

    @pl.loop(1, 8)
    def _(r):
        group_ask(r).start()

    part = ask_mid.at[pl.ds(1, 7)]
    pltpu.make_async_copy(part, part, ask_sems.at[0]).wait()
    ask_sum[...] = jnp.sum(ask_mid[...], axis=0)

    @pl.loop(1, 16)
    def _(p):
        plane_ask(p).start()

    asked[0] = ask_sum[0]
    part = asked.at[pl.ds(1, 15)]
    pltpu.make_async_copy(part, part, ask_sems.at[1]).wait()

    def wait_chunk(buffer, sems, c):
        @pl.when(c == 0)
        def _():
            part = buffer.at[pl.ds(1, GROUP - 1)]
            pltpu.make_async_copy(part, part, sems.at[0]).wait()

        @pl.when(c > 0)
        def _():
            part = buffer.at[pl.ds(c * GROUP, GROUP)]
            pltpu.make_async_copy(part, part, sems.at[c]).wait()

    def row_copy(i):
        return remote(
            row_send.at[i],
            rows.at[i],
            send_sems.at[1],
            row_sems.at[i // GROUP],
            behind(i),
        )

    @pl.loop(0, CHUNKS)
    def _(c):
        parts = []
        for g in range(GROUP):
            dx, dy, dz, dc = deltas(c * GROUP + g)
            line = jnp.broadcast_to(asked[dx * 4 + dz], (PAD, LANES))
            lane = iota((PAD, LANES), 1) - (dc * 4 + dy) * PAD
            parts.append(jnp.where(lane == iota((PAD, LANES), 0), line, 0.0))
        index = jnp.sum(jnp.concatenate(parts, axis=0), axis=1, keepdims=True)
        index_col[pl.ds(pl.multiple_of(c * SLOTS, SLOTS), SLOTS), :] = index
        pick = onehot(index.astype(jnp.int32) == iota((SLOTS, rows_here), 1))
        picked = dot(pick, table_high[...], 1, 1) + dot(pick, table_low[...], 1, 1)
        pack(row_send, c, picked)

        @pl.when(c == 0)
        def _():
            rows[0] = row_send[0]

        @pl.loop(0, GROUP)
        def _(g):
            @pl.when(c * GROUP + g > 0)
            def _():
                row_copy(c * GROUP + g).start()

    rel_acc[...] = jnp.zeros_like(rel_acc)
    for half in range(REL_PARTS):
        load_relations(half).wait()

        @pl.loop(0, rel_cuts[half + 1] - rel_cuts[half])
        def _(t):
            high, low = split(relations[:, pl.ds(pl.multiple_of(t * REL, REL), REL)])
            base = (t + rel_cuts[half]) * REL
            pick = onehot(iota((REL, edges), 0) + base == rels[...])
            found = dot(jnp.concatenate([high, low], axis=0), pick, 1, 0)
            rel_acc[...] += found[0:width] + found[width:]

        if half + 1 < REL_PARTS:
            load_relations(half + 1).start()

    rel_rows[...] = jnp.zeros_like(rel_rows)
    rel_rows[:, 0:width] = rel_acc[...].T

    @pl.loop(0, CHUNKS)
    def _(c):
        wait_chunk(rows, row_sems, c)
        high, low = split(unpack(rows, c))
        place = onehot(slot_col[...].astype(jnp.int32) - c * SLOTS == iota((count, SLOTS), 1))
        wanted[...] += dot(place, high, 1, 0) + dot(place, low, 1, 0)

    high, low = split(wanted[:, body:])
    fold = onehot(lax.rem(iota((LANES, LANES), 0), TAIL) == iota((LANES, LANES), 1))
    wanted[:, body:] = dot(high, fold, 1, 0) + dot(low, fold, 1, 0)
    queries = wanted[0:edges, :] + rel_rows[...]
    residue = queries - wanted[edges : 2 * edges, :]
    pos_dist = jnp.sqrt(jnp.sum(residue * residue, axis=1, keepdims=True) + EPSILON)
    grad_pos = (1.0 / (1.0 + jnp.exp(MARGIN - pos_dist)) / pos_dist) * residue
    all_queries[0, 0] = to_lines(queries)

    sibling = (dp, blk + 1 - 2 * mc)

    def at_y(dy):
        return dp, lax.rem(my + dy, 4) * 2 + mc

    def half_copy(dy, half):
        lines = pl.ds(half * (width // 2), width // 2)
        return remote(
            all_queries.at[0, 0, lines, :],
            all_queries.at[dy, 0, lines, :],
            half_send_sems.at[dy, half],
            half_sems.at[dy, half],
            at_y(dy),
        )

    def relay_copy(half):
        lines = pl.ds(half * (width // 2), width // 2)
        return remote(
            all_queries.at[1 + 2 * half, 0, lines, :],
            all_queries.at[2, 0, lines, :],
            half_send_sems.at[2, half],
            half_sems.at[2, half],
            at_y(1 + 2 * half),
        )

    def forward_copy(dy):
        return remote(
            all_queries.at[dy, 0],
            all_queries.at[dy, 1],
            query_send_sems.at[dy],
            query_sems.at[dy],
            sibling,
        )

    for dy, half in ((1, 0), (3, 1), (1, 1), (3, 0)):
        half_copy(dy, half).start()
    forward_copy(0).start()
    negatives = wanted[2 * edges :, :]
    high, low = split(negatives)
    neg_pieces[0] = high
    neg_pieces[1] = low
    neg_col = jnp.sum(negatives * negatives, axis=1, keepdims=True)
    neg_count = negatives.shape[0]
    neg_sq = jnp.concatenate(
        [to_row(neg_col[128 * t : 128 * t + 128]) for t in range(neg_count // 128)], axis=1
    )
    block_acc[...] = jnp.zeros_like(block_acc)
    coef_cols[...] = jnp.zeros_like(coef_cols)
    weight = 8.0 * neg_count

    def sibling_copy(dy):
        return remote(
            parts.at[dy, 1],
            part_sibling.at[dy],
            part_send_sems.at[dy, 0],
            part_sems.at[dy, 0],
            sibling,
        )

    def home_copy(dy):
        return remote(
            part_sum.at[dy],
            part_recv.at[dy],
            part_send_sems.at[dy, 1],
            part_sems.at[dy, 1],
            (dp, lax.rem(my + 4 - dy, 4) * 2 + mc),
        )

    def block_terms(block, where):
        pieces = split(block)
        block_sq = jnp.sum(block * block, axis=1, keepdims=True)
        neg_parts = (neg_pieces[0], neg_pieces[1])
        both = dot(jnp.concatenate(pieces, axis=0), neg_parts[0], 1, 1)
        inner = both[0:edges] + (both[edges:] + dot(pieces[0], neg_parts[1], 1, 1))
        dist = jnp.sqrt(block_sq + neg_sq - 2.0 * inner + EPSILON)
        coef = -1.0 / ((1.0 + jnp.exp(dist - MARGIN)) * (weight * dist))
        coef_parts = split(coef)
        coef_cols[...] += jnp.sum(coef, axis=0, keepdims=True)
        block_acc[...] += dot3(coef_parts, pieces, 0, 0)
        both = dot(jnp.concatenate(coef_parts, axis=0), neg_parts[0], 1, 0)
        drawn = both[0:edges] + (both[edges:] + dot(coef_parts[0], neg_parts[1], 1, 0))
        return block * jnp.sum(coef, axis=1, keepdims=True) - drawn

    def finish(dy):
        sibling_copy(dy).wait_recv()
        part_sum[dy] = parts[dy, 0] + part_sibling[dy]

    @pl.loop(0, 8)
    def _(u):
        v, w = u // 2, lax.rem(u, 2)
        far = (v + 1) // 2
        dy = far + lax.rem(far, 2) * 2 * w
        dc = v // 2 + (1 - (lax.rem(v, 3) + 1) // 2) * w * (1 - 2 * (v // 2))

        @pl.when(u == 2)
        def _():
            half_copy(1, 0).wait_recv()
            relay_copy(0).start()
            half_copy(3, 1).wait_recv()
            relay_copy(1).start()
            half_copy(1, 1).wait_recv()
            forward_copy(1).start()
            half_copy(3, 0).wait_recv()
            forward_copy(3).start()

        @pl.when(u == 4)
        def _():
            relay_copy(0).wait_recv()
            relay_copy(1).wait_recv()
            forward_copy(2).start()

        @pl.when(dc == 1)
        def _():
            forward_copy(dy).wait_recv()

        where = pl.ds(pl.multiple_of(u * edges, edges), edges)
        parts[dy, dc] = to_lines(block_terms(from_lines(all_queries[dy, dc]), where))

        @pl.when(dc == 1)
        def _():
            sibling_copy(dy).start()

        @pl.when((u == 5) | (u == 6))
        def _():
            last = 1 + 2 * (u - 5)
            finish(last)
            home_copy(last).start()

    finish(2)
    home_copy(2).start()
    finish(0)
    coef_col = jnp.concatenate(
        [to_column(coef_cols[:, 128 * t : 128 * t + 128]) for t in range(neg_count // 128)], axis=0
    )
    spread = onehot(iota((LANES, LANES), 0) == lax.rem(iota((LANES, LANES), 1), TAIL))

    def keep(first, last, value):
        for n, piece in enumerate(split(value)):
            grad_pieces[n, first:last, 0:body] = piece[:, 0:body]
            grad_pieces[n, first:last, body:] = dot(piece[:, body:], spread, 1, 0).astype(BF16)

    keep(edges, 2 * edges, -grad_pos)
    keep(2 * edges, count, wanted[2 * edges :, :] * coef_col - block_acc[...])
    for dy in (1, 3, 2):
        home_copy(dy).wait_recv()
    grad_neg = from_lines((part_sum[0] + part_recv[1]) + (part_recv[2] + part_recv[3]))
    keep(0, edges, grad_pos + grad_neg)

    def grad_copy(i):
        return remote(
            grad_send.at[i],
            grads.at[i],
            send_sems.at[2],
            grad_sems.at[i // GROUP],
            ahead(i),
        )

    @pl.loop(0, CHUNKS)
    def _(c):
        line = iota((SLOTS, LANES), 0)
        base = line + c * SLOTS - jnp.where(lax.rem(line, PAD) < CAP, 0, PAD - CAP)
        place = jnp.concatenate(
            [onehot(slot_row[t : t + 1, :].astype(jnp.int32) == base) for t in range(6)], axis=1
        )
        packed = dot(place, grad_pieces[0], 1, 0) + dot(place, grad_pieces[1], 1, 0)
        pack(grad_send, c, packed)

        @pl.when(c == 0)
        def _():
            grads[0] = grad_send[0]

        @pl.loop(0, GROUP)
        def _(g):
            @pl.when(c * GROUP + g > 0)
            def _():
                grad_copy(c * GROUP + g).start()

    @pl.loop(0, CHUNKS)
    def _(c):
        wait_chunk(grads, grad_sems, c)
        high, low = split(unpack(grads, c).T)
        index = index_col[pl.ds(pl.multiple_of(c * SLOTS, SLOTS), SLOTS), :].astype(jnp.int32)
        used = lax.rem(iota((SLOTS, 1), 0), PAD) < CAP
        pick = onehot(jnp.where(used, index, -1) == iota((SLOTS, rows_here), 1))
        summed[...] += dot(high, pick, 1, 0) + dot(low, pick, 1, 0)

    tail = summed[body:width]
    for j in range(1, LANES // TAIL):
        tail = tail + summed[body + TAIL * j : body + TAIL * j + TAIL]
    total = jnp.concatenate([summed[0:body], tail], axis=0)
    new_sum = adagrad[...] + jnp.sum(total * total, axis=0, keepdims=True) * (1.0 / width)
    sum_out[...] = new_sum
    table_out[...] = table[...] - total * (LEARNING_RATE / jnp.sqrt(new_sum))

    part = ask_send.at[pl.ds(1, 7)]
    pltpu.make_async_copy(part, part, send_sems.at[0]).wait()
    part = asked.at[pl.ds(1, 15)]
    pltpu.make_async_copy(part, part, send_sems.at[3]).wait()
    for n, buffer in ((1, row_send), (2, grad_send)):
        part = buffer.at[pl.ds(1, DEVICES - 1)]
        pltpu.make_async_copy(part, part, send_sems.at[n]).wait()
    for dy in range(4):
        forward_copy(dy).wait_send()
        sibling_copy(dy).wait_send()
        if dy > 0:
            home_copy(dy).wait_send()
    for half in range(2):
        half_copy(1, half).wait_send()
        half_copy(3, half).wait_send()
        relay_copy(half).wait_send()


def on_device(entity_table, adagrad_sum, relations, owner_map, head_ids, rel_ids, tail_ids, neg_ids):
    rows_here, width = entity_table.shape
    edges = head_ids.shape[0]
    neg_count = neg_ids.shape[0]
    count = 2 * edges + neg_count
    map_rows = owner_map.shape[0] // 128
    vmem = pl.BlockSpec(memory_space=pltpu.VMEM)
    hbm = pl.BlockSpec(memory_space=pltpu.HBM)
    wide = 4 * LANES
    slots = pltpu.VMEM((DEVICES, LINES, LANES), F32)
    parts = pltpu.VMEM((4, width, LANES), F32)
    sem = pltpu.SemaphoreType.DMA
    new_table, new_sum = pl.pallas_call(
        step_kernel,
        out_shape=(
            jax.ShapeDtypeStruct((width, rows_here), F32),
            jax.ShapeDtypeStruct((1, rows_here), F32),
        ),
        in_specs=[hbm] * 8,
        out_specs=(vmem, vmem),
        scratch_shapes=[
            pltpu.VMEM((1, edges), jnp.int32),
            pltpu.VMEM((1, edges), jnp.int32),
            pltpu.VMEM((neg_count // LANES, LANES), jnp.int32),
            pltpu.VMEM((1, edges), jnp.int32),
            pltpu.VMEM((1, rows_here), F32),
            pltpu.VMEM((map_rows, 128), jnp.int32),
            pltpu.VMEM((width, rows_here), F32),
            pltpu.VMEM((width, -(-relations.shape[0] // (REL * REL_PARTS)) * REL), F32),
            pltpu.VMEM((map_rows, 384), BF16),
            pltpu.VMEM((wide, rows_here), BF16),
            pltpu.VMEM((wide, rows_here), BF16),
            pltpu.VMEM((8, 128), jnp.int32),
            pltpu.VMEM((count, 1), F32),
            pltpu.VMEM((count, 1), F32),
            pltpu.VMEM((count, 1), F32),
            pltpu.VMEM((count, 1), F32),
            pltpu.VMEM((8, 128), F32),
            pltpu.VMEM((8, 16, 1, LANES), F32),
            pltpu.VMEM((8, 16, 1, LANES), F32),
            pltpu.VMEM((16, 1, LANES), F32),
            pltpu.VMEM((16, 1, LANES), F32),
            pltpu.VMEM((DEVICES * PAD, 1), F32),
            slots,
            slots,
            pltpu.VMEM((count, wide), F32),
            pltpu.VMEM((width, edges), F32),
            pltpu.VMEM((edges, wide), F32),
            pltpu.VMEM((2, neg_count, wide), BF16),
            pltpu.VMEM((neg_count, wide), F32),
            pltpu.VMEM((1, neg_count), F32),
            pltpu.VMEM((4, 2, width, LANES), F32),
            pltpu.VMEM((4, 2, width, LANES), F32),
            parts,
            parts,
            parts,
            pltpu.VMEM((2, count, wide), BF16),
            slots,
            slots,
            pltpu.VMEM((wide, rows_here), F32),
            sem((8,)),
            sem((2,)),
            sem((CHUNKS,)),
            sem((CHUNKS,)),
            sem((4, 2)),
            sem((4,)),
            sem((4, 2)),
            sem((4,)),
            sem((4, 2)),
            sem((4,)),
            sem((4, 2)),
        ],
        compiler_params=pltpu.CompilerParams(
            collective_id=0, has_side_effects=True, vmem_limit_bytes=LIMIT
        ),
    )(
        pltpu.with_memory_space_constraint(head_ids.reshape(1, edges), pltpu.HBM),
        pltpu.with_memory_space_constraint(tail_ids.reshape(1, edges), pltpu.HBM),
        pltpu.with_memory_space_constraint(neg_ids.reshape(neg_count // 128, 128), pltpu.HBM),
        pltpu.with_memory_space_constraint(rel_ids.reshape(1, edges), pltpu.HBM),
        pltpu.with_memory_space_constraint(owner_map.reshape(map_rows, 128), pltpu.HBM),
        pltpu.with_memory_space_constraint(entity_table.T, pltpu.HBM),
        pltpu.with_memory_space_constraint(relations.T, pltpu.HBM),
        pltpu.with_memory_space_constraint(adagrad_sum.reshape(1, rows_here), pltpu.HBM),
    )
    return new_table.T, new_sum.reshape(rows_here)


def solution(mesh):
    assert dict(mesh.shape) == {"dp": 16, "blk": 8}
    return jax.shard_map(
        on_device,
        mesh=mesh,
        in_specs=(
            P(("dp", "blk"), None),
            P(("dp", "blk")),
            P(),
            P(),
            P(("dp", "blk")),
            P(("dp", "blk")),
            P(("dp", "blk")),
            P(("dp", "blk")),
        ),
        out_specs=(P(("dp", "blk"), None), P(("dp", "blk"))),
        check_vma=False,
    )
```

```python
import functools

import jax
import jax.numpy as jnp
from jax import lax
from jax.experimental import pallas as pl
from jax.experimental.pallas import tpu as pltpu
from jax.sharding import PartitionSpec as P

MARGIN = 10.0
EPSILON = 1e-05
LEARNING_RATE = 0.1
MESH = pl.DeviceIdType.MESH
F32 = jnp.float32
BF16 = jnp.bfloat16
DEVICES = 128
CAP = 12
PAD = 16
GROUP = 16
CHUNKS = DEVICES // GROUP
SLOTS = GROUP * PAD
LINES = 40
LIMIT = 50 * 1024 * 1024
LANES = 128
TAIL = 16
REL = 256
REL_PARTS = 3


def split(x):
    high = x.astype(BF16)
    return high, (x - high.astype(F32)).astype(BF16)


def dot(a, b, ca, cb):
    return lax.dot_general(a, b, (((ca,), (cb,)), ((), ())), preferred_element_type=F32)


def dot3(a, b, ca, cb):
    return dot(a[0], b[0], ca, cb) + (dot(a[0], b[1], ca, cb) + dot(a[1], b[0], ca, cb))


def iota(shape, axis):
    return lax.broadcasted_iota(jnp.int32, shape, axis)


def onehot(mask):
    return jnp.where(mask, 1.0, 0.0).astype(BF16)


def to_column(row):
    n = row.shape[1]
    return jnp.sum(jnp.where(iota((n, n), 0) == iota((n, n), 1), row, 0.0), axis=1, keepdims=True)


def to_row(column):
    n = column.shape[0]
    return jnp.sum(jnp.where(iota((n, n), 0) == iota((n, n), 1), column, 0.0), axis=0, keepdims=True)


def tail_mask():
    return iota((GROUP, 8, LANES), 1) == iota((GROUP, 8, LANES), 2) // TAIL


def pack(buffer, c, full):
    full = full.reshape(GROUP, PAD, 4 * LANES)
    up, low = full[:, 0:8], full[:, 8:16]
    sub = iota((GROUP, 8, LANES), 1)
    first = sub < 4
    tail_up = jnp.sum(jnp.where(tail_mask(), up[:, :, 3 * LANES :], 0.0), axis=1, keepdims=True)
    tail_low = jnp.sum(
        jnp.where(tail_mask() & first, low[:, :, 3 * LANES :], 0.0), axis=1, keepdims=True
    )
    here = pl.ds(c * GROUP, GROUP)
    for n in range(3):
        buffer[here, 8 * n : 8 * n + 8, :] = up[:, :, LANES * n : LANES * n + LANES]
    buffer[here, 24:32, :] = jnp.where(first, low[:, :, 0:LANES], low[:, :, LANES : 2 * LANES])
    rest = jnp.where(sub == 4, tail_up, jnp.where(sub == 5, tail_low, 0.0))
    buffer[here, 32:40, :] = jnp.where(first, low[:, :, 2 * LANES : 3 * LANES], rest)


def unpack(buffer, c):
    part = buffer[pl.ds(c * GROUP, GROUP)]
    lines = [part[:, 8 * n : 8 * n + 8] for n in range(5)]
    first = iota((GROUP, 8, LANES), 1) < 4
    tail_up = jnp.where(tail_mask(), lines[4][:, 4:5], 0.0)
    tail_low = jnp.where(tail_mask() & first, lines[4][:, 5:6], 0.0)
    turned = pltpu.roll(lines[3].reshape(GROUP * 8, LANES), GROUP * 8 - 4, 0)
    turned = turned.reshape(GROUP, 8, LANES)
    up = jnp.concatenate([lines[0], lines[1], lines[2], tail_up], axis=2)
    low = jnp.concatenate([lines[3], turned, lines[4], tail_low], axis=2)
    return jnp.concatenate([up, low], axis=1).reshape(SLOTS, 4 * LANES)


def to_lines(x):
    tail = x[:, 3 * LANES :]
    for shift in (TAIL, 2 * TAIL, 4 * TAIL):
        tail = tail + pltpu.roll(tail, shift, 1)
    tail = tail.reshape(GROUP, 8, LANES)
    tail = jnp.sum(jnp.where(tail_mask(), tail, 0.0), axis=1)
    return jnp.concatenate([x[:, LANES * n : LANES * n + LANES] for n in range(3)] + [tail], axis=0)


def from_lines(lines):
    tail = lines[3 * LANES :].reshape(GROUP, 1, LANES)
    tail = jnp.where(tail_mask(), tail, 0.0).reshape(LANES, LANES)
    for shift in (4 * TAIL, 2 * TAIL, TAIL):
        tail = tail + pltpu.roll(tail, shift, 1)
    tail = jnp.where(iota((LANES, LANES), 1) < TAIL, tail, 0.0)
    return jnp.concatenate([lines[LANES * n : LANES * n + LANES] for n in range(3)] + [tail], axis=1)


def step_kernel(
    heads_hbm,
    tails_hbm,
    negs_hbm,
    rels_hbm,
    map_hbm,
    table_hbm,
    relations_hbm,
    adagrad_hbm,
    table_out,
    sum_out,
    heads,
    tails,
    negs,
    rels,
    adagrad,
    map_ref,
    table,
    relations,
    map_parts,
    table_high,
    table_low,
    ids,
    key_col,
    ask_col,
    local_col,
    slot_col,
    slot_row,
    ask_send,
    ask_mid,
    ask_sum,
    asked,
    index_col,
    row_send,
    rows,
    wanted,
    rel_acc,
    rel_rows,
    neg_pieces,
    block_acc,
    coef_cols,
    all_queries,
    parts,
    part_sibling,
    part_sum,
    part_recv,
    grad_pieces,
    grad_send,
    grads,
    summed,
    load_sem,
    ask_sems,
    row_sems,
    grad_sems,
    half_sems,
    query_sems,
    part_sems,
    send_sems,
    half_send_sems,
    query_send_sems,
    part_send_sems,
):
    dp = lax.axis_index("dp")
    blk = lax.axis_index("blk")
    mx, mz = dp // 4, lax.rem(dp, 4)
    my, mc = blk // 2, lax.rem(blk, 2)
    width = table.shape[0]
    body = 3 * LANES
    rows_here = table.shape[1]
    edges = heads.shape[1]
    rel_chunks = relations_hbm.shape[1] // REL
    rel_step = relations.shape[1] // REL
    rel_cuts = [min(n * rel_step, rel_chunks) for n in range(REL_PARTS + 1)]

    def deltas(i):
        a, b, c, dc = lax.rem(i, 4), lax.rem(i // 4, 4), lax.rem(i // 16, 4), i // 64
        return a, lax.rem(a + b, 4), lax.rem(a + c, 4), dc

    def ahead(i):
        dx, dy, dz, dc = deltas(i)
        return (
            lax.rem(mx + dx, 4) * 4 + lax.rem(mz + dz, 4),
            lax.rem(my + dy, 4) * 2 + lax.rem(mc + dc, 2),
        )

    def behind(i):
        dx, dy, dz, dc = deltas(i)
        return (
            lax.rem(mx + 4 - dx, 4) * 4 + lax.rem(mz + 4 - dz, 4),
            lax.rem(my + 4 - dy, 4) * 2 + lax.rem(mc + dc, 2),
        )

    def remote(src, dst, send, recv, device):
        return pltpu.make_async_remote_copy(
            src_ref=src,
            dst_ref=dst,
            send_sem=send,
            recv_sem=recv,
            device_id=device,
            device_id_type=MESH,
        )

    load_map = pltpu.make_async_copy(map_hbm, map_ref, load_sem.at[0])
    load_table = pltpu.make_async_copy(table_hbm, table, load_sem.at[1])

    def load_relations(half):
        first, lanes = rel_cuts[half] * REL, (rel_cuts[half + 1] - rel_cuts[half]) * REL
        part = relations_hbm.at[:, pl.ds(first, lanes)]
        return pltpu.make_async_copy(part, relations.at[:, pl.ds(0, lanes)], load_sem.at[2])

    small = [
        pltpu.make_async_copy(src, dst, load_sem.at[3 + n])
        for n, (src, dst) in enumerate(
            [
                (heads_hbm, heads),
                (tails_hbm, tails),
                (negs_hbm, negs),
                (rels_hbm, rels),
                (adagrad_hbm, adagrad),
            ]
        )
    ]
    for copy in small:
        copy.start()
    load_map.start()
    load_table.start()
    load_relations(0).start()
    barrier = pltpu.get_barrier_semaphore()

    def in_group(r):
        return dp, lax.rem(my + lax.rem(r, 4), 4) * 2 + lax.rem(mc + r // 4, 2)

    def in_plane(p):
        return lax.rem(mx + p // 4, 4) * 4 + lax.rem(mz + lax.rem(p, 4), 4), blk

    @pl.loop(1, 8)
    def _(r):
        pl.semaphore_signal(barrier, inc=1, device_id=in_group(r), device_id_type=MESH)

    @pl.loop(1, 16)
    def _(p):
        pl.semaphore_signal(barrier, inc=1, device_id=in_plane(p), device_id_type=MESH)

    for copy in small:
        copy.wait()
    ids[0:1, :] = heads[...]
    ids[1:2, :] = tails[...]
    ids[2:6, :] = negs[...]
    load_map.wait()
    position_of = map_ref[...]
    map_parts[:, 0:128] = (position_of & 255).astype(F32).astype(BF16)
    map_parts[:, 128:256] = ((position_of >> 8) & 255).astype(F32).astype(BF16)
    map_parts[:, 256:384] = (position_of >> 16).astype(F32).astype(BF16)

    @pl.loop(0, 6)
    def _(t):
        column = to_column(ids[pl.ds(t, 1), :].astype(F32)).astype(jnp.int32)
        line = onehot((column >> 7) == iota((128, map_ref.shape[0]), 1))
        found = dot(line, map_parts[...], 1, 0)
        lane = (column & 127) == iota((128, 128), 1)
        piece = [
            jnp.sum(jnp.where(lane, found[:, 128 * p : 128 * p + 128], 0.0), axis=1, keepdims=True)
            for p in range(3)
        ]
        position = (piece[0] + 256.0 * piece[1] + 65536.0 * piece[2]).astype(jnp.int32)
        owner = position >> 11
        dx = ((owner >> 5) - mx) & 3
        dz = ((owner >> 3) - mz) & 3
        dy = ((owner >> 1) - my) & 3
        dc = (owner - mc) & 1
        key = dc * 64 + ((dz - dx) & 3) * 16 + ((dy - dx) & 3) * 4 + dx
        ask = (dc * 4 + dy) * 16 + dx * 4 + dz
        where = pl.ds(pl.multiple_of(t * 128, 128), 128)
        key_col[where, :] = key.astype(F32)
        ask_col[where, :] = ask.astype(F32)
        local_col[where, :] = (position & (rows_here - 1)).astype(F32)

    count = key_col.shape[0]
    keys = key_col[...]
    key_hot = onehot(ask_col[...].astype(jnp.int32) == iota((count, DEVICES), 1))
    earlier = onehot(iota((count, count), 1) < iota((count, count), 0))
    before = dot(earlier, key_hot, 1, 0)
    rank = jnp.sum(before * key_hot.astype(F32), axis=1, keepdims=True)
    local = local_col[...].astype(jnp.int32)
    place = rank.astype(jnp.int32)
    lane = iota((count, LANES), 1)
    spread = lane - (ask_col[...].astype(jnp.int32) // 16) * PAD
    spot = (place == spread) | ((place >= 8) & (place + 4 == spread))
    upper = jnp.where(spot, (local >> 8).astype(F32), 0.0).astype(BF16)
    lower = jnp.where(spot, (local & 255).astype(F32), 0.0).astype(BF16)
    asks = 256.0 * dot(key_hot, upper, 0, 0) + dot(key_hot, lower, 0, 0)
    ask_send[...] = asks.reshape(8, 16, 1, LANES)
    slot = keys * float(PAD) + rank
    slot_col[...] = slot
    for t in range(6):
        slot_row[t : t + 1, :] = to_row(slot[128 * t : 128 * t + 128])

    ask_mid[0] = ask_send[0]

    pl.semaphore_wait(barrier, 22)

    def group_ask(r):
        return remote(ask_send.at[r], ask_mid.at[r], send_sems.at[0], ask_sems.at[0], in_group(r))

    def plane_ask(p):
        return remote(ask_sum.at[p], asked.at[p], send_sems.at[3], ask_sems.at[1], in_plane(p))

    @pl.loop(1, 8)
    def _(r):
        group_ask(r).start()

    load_table.wait()
    high, low = split(table[...])
    table_high[0:width] = high
    table_low[0:width] = low
    for j in range(1, LANES // TAIL):
        table_high[body + TAIL * j : body + TAIL * j + TAIL] = high[body:]
        table_low[body + TAIL * j : body + TAIL * j + TAIL] = low[body:]
    summed[...] = jnp.zeros_like(summed)
    wanted[...] = jnp.zeros_like(wanted)
    part = ask_mid.at[pl.ds(1, 7)]
    pltpu.make_async_copy(part, part, ask_sems.at[0]).wait()
    ask_sum[...] = jnp.sum(ask_mid[...], axis=0)

    @pl.loop(1, 16)
    def _(p):
        plane_ask(p).start()

    asked[0] = ask_sum[0]
    part = asked.at[pl.ds(1, 15)]
    pltpu.make_async_copy(part, part, ask_sems.at[1]).wait()

    def wait_chunk(buffer, sems, c):
        @pl.when(c == 0)
        def _():
            part = buffer.at[pl.ds(1, GROUP - 1)]
            pltpu.make_async_copy(part, part, sems.at[0]).wait()

        @pl.when(c > 0)
        def _():
            part = buffer.at[pl.ds(c * GROUP, GROUP)]
            pltpu.make_async_copy(part, part, sems.at[c]).wait()

    def row_copy(i):
        return remote(
            row_send.at[i],
            rows.at[i],
            send_sems.at[1],
            row_sems.at[i // GROUP],
            behind(i),
        )

    @pl.loop(0, CHUNKS)
    def _(c):
        parts = []
        for g in range(GROUP):
            dx, dy, dz, dc = deltas(c * GROUP + g)
            line = jnp.broadcast_to(asked[dx * 4 + dz], (PAD, LANES))
            lane = iota((PAD, LANES), 1) - (dc * 4 + dy) * PAD
            parts.append(jnp.where(lane == iota((PAD, LANES), 0), line, 0.0))
        index = jnp.sum(jnp.concatenate(parts, axis=0), axis=1, keepdims=True)
        index_col[pl.ds(pl.multiple_of(c * SLOTS, SLOTS), SLOTS), :] = index
        pick = onehot(index.astype(jnp.int32) == iota((SLOTS, rows_here), 1))
        picked = dot(pick, table_high[...], 1, 1) + dot(pick, table_low[...], 1, 1)
        pack(row_send, c, picked)

        @pl.when(c == 0)
        def _():
            rows[0] = row_send[0]

        @pl.loop(0, GROUP)
        def _(g):
            @pl.when(c * GROUP + g > 0)
            def _():
                row_copy(c * GROUP + g).start()

    rel_acc[...] = jnp.zeros_like(rel_acc)
    for half in range(REL_PARTS):
        load_relations(half).wait()

        @pl.loop(0, rel_cuts[half + 1] - rel_cuts[half])
        def _(t):
            high, low = split(relations[:, pl.ds(pl.multiple_of(t * REL, REL), REL)])
            base = (t + rel_cuts[half]) * REL
            pick = onehot(iota((REL, edges), 0) + base == rels[...])
            found = dot(jnp.concatenate([high, low], axis=0), pick, 1, 0)
            rel_acc[...] += found[0:width] + found[width:]

        if half + 1 < REL_PARTS:
            load_relations(half + 1).start()

    rel_rows[...] = jnp.zeros_like(rel_rows)
    rel_rows[:, 0:width] = rel_acc[...].T

    @pl.loop(0, CHUNKS)
    def _(c):
        wait_chunk(rows, row_sems, c)
        high, low = split(unpack(rows, c))
        place = onehot(slot_col[...].astype(jnp.int32) - c * SLOTS == iota((count, SLOTS), 1))
        wanted[...] += dot(place, high, 1, 0) + dot(place, low, 1, 0)

    high, low = split(wanted[:, body:])
    fold = onehot(lax.rem(iota((LANES, LANES), 0), TAIL) == iota((LANES, LANES), 1))
    wanted[:, body:] = dot(high, fold, 1, 0) + dot(low, fold, 1, 0)
    queries = wanted[0:edges, :] + rel_rows[...]
    residue = queries - wanted[edges : 2 * edges, :]
    pos_dist = jnp.sqrt(jnp.sum(residue * residue, axis=1, keepdims=True) + EPSILON)
    grad_pos = (1.0 / (1.0 + jnp.exp(MARGIN - pos_dist)) / pos_dist) * residue
    all_queries[0, 0] = to_lines(queries)

    sibling = (dp, blk + 1 - 2 * mc)

    def at_y(dy):
        return dp, lax.rem(my + dy, 4) * 2 + mc

    def half_copy(dy, half):
        lines = pl.ds(half * (width // 2), width // 2)
        return remote(
            all_queries.at[0, 0, lines, :],
            all_queries.at[dy, 0, lines, :],
            half_send_sems.at[dy, half],
            half_sems.at[dy, half],
            at_y(dy),
        )

    def relay_copy(half):
        lines = pl.ds(half * (width // 2), width // 2)
        return remote(
            all_queries.at[1 + 2 * half, 0, lines, :],
            all_queries.at[2, 0, lines, :],
            half_send_sems.at[2, half],
            half_sems.at[2, half],
            at_y(1 + 2 * half),
        )

    def forward_copy(dy):
        return remote(
            all_queries.at[dy, 0],
            all_queries.at[dy, 1],
            query_send_sems.at[dy],
            query_sems.at[dy],
            sibling,
        )

    for dy, half in ((1, 0), (3, 1), (1, 1), (3, 0)):
        half_copy(dy, half).start()
    forward_copy(0).start()
    negatives = wanted[2 * edges :, :]
    high, low = split(negatives)
    neg_pieces[0] = high
    neg_pieces[1] = low
    neg_col = jnp.sum(negatives * negatives, axis=1, keepdims=True)
    neg_count = negatives.shape[0]
    neg_sq = jnp.concatenate(
        [to_row(neg_col[128 * t : 128 * t + 128]) for t in range(neg_count // 128)], axis=1
    )
    block_acc[...] = jnp.zeros_like(block_acc)
    coef_cols[...] = jnp.zeros_like(coef_cols)
    weight = 8.0 * neg_count

    def sibling_copy(dy):
        return remote(
            parts.at[dy, 1],
            part_sibling.at[dy],
            part_send_sems.at[dy, 0],
            part_sems.at[dy, 0],
            sibling,
        )

    def home_copy(dy):
        return remote(
            part_sum.at[dy],
            part_recv.at[dy],
            part_send_sems.at[dy, 1],
            part_sems.at[dy, 1],
            (dp, lax.rem(my + 4 - dy, 4) * 2 + mc),
        )

    def block_terms(block, where):
        pieces = split(block)
        block_sq = jnp.sum(block * block, axis=1, keepdims=True)
        neg_parts = (neg_pieces[0], neg_pieces[1])
        both = dot(jnp.concatenate(pieces, axis=0), neg_parts[0], 1, 1)
        inner = both[0:edges] + (both[edges:] + dot(pieces[0], neg_parts[1], 1, 1))
        dist = jnp.sqrt(block_sq + neg_sq - 2.0 * inner + EPSILON)
        coef = -1.0 / ((1.0 + jnp.exp(dist - MARGIN)) * (weight * dist))
        coef_parts = split(coef)
        coef_cols[...] += jnp.sum(coef, axis=0, keepdims=True)
        block_acc[...] += dot3(coef_parts, pieces, 0, 0)
        both = dot(jnp.concatenate(coef_parts, axis=0), neg_parts[0], 1, 0)
        drawn = both[0:edges] + (both[edges:] + dot(coef_parts[0], neg_parts[1], 1, 0))
        return block * jnp.sum(coef, axis=1, keepdims=True) - drawn

    def finish(dy):
        sibling_copy(dy).wait_recv()
        part_sum[dy] = parts[dy, 0] + part_sibling[dy]

    @pl.loop(0, 8)
    def _(u):
        v, w = u // 2, lax.rem(u, 2)
        far = (v + 1) // 2
        dy = far + lax.rem(far, 2) * 2 * w
        dc = v // 2 + (1 - (lax.rem(v, 3) + 1) // 2) * w * (1 - 2 * (v // 2))

        @pl.when(u == 2)
        def _():
            half_copy(1, 0).wait_recv()
            relay_copy(0).start()
            half_copy(3, 1).wait_recv()
            relay_copy(1).start()
            half_copy(1, 1).wait_recv()
            forward_copy(1).start()
            half_copy(3, 0).wait_recv()
            forward_copy(3).start()

        @pl.when(u == 4)
        def _():
            relay_copy(0).wait_recv()
            relay_copy(1).wait_recv()
            forward_copy(2).start()

        @pl.when(dc == 1)
        def _():
            forward_copy(dy).wait_recv()

        where = pl.ds(pl.multiple_of(u * edges, edges), edges)
        parts[dy, dc] = to_lines(block_terms(from_lines(all_queries[dy, dc]), where))

        @pl.when(dc == 1)
        def _():
            sibling_copy(dy).start()

        @pl.when((u == 5) | (u == 6))
        def _():
            last = 1 + 2 * (u - 5)
            finish(last)
            home_copy(last).start()

    finish(2)
    home_copy(2).start()
    finish(0)
    coef_col = jnp.concatenate(
        [to_column(coef_cols[:, 128 * t : 128 * t + 128]) for t in range(neg_count // 128)], axis=0
    )
    spread = onehot(iota((LANES, LANES), 0) == lax.rem(iota((LANES, LANES), 1), TAIL))

    def keep(first, last, value):
        for n, piece in enumerate(split(value)):
            grad_pieces[n, first:last, 0:body] = piece[:, 0:body]
            grad_pieces[n, first:last, body:] = dot(piece[:, body:], spread, 1, 0).astype(BF16)

    keep(edges, 2 * edges, -grad_pos)
    keep(2 * edges, count, wanted[2 * edges :, :] * coef_col - block_acc[...])
    for dy in (1, 3, 2):
        home_copy(dy).wait_recv()
    grad_neg = from_lines((part_sum[0] + part_recv[1]) + (part_recv[2] + part_recv[3]))
    keep(0, edges, grad_pos + grad_neg)

    def grad_copy(i):
        return remote(
            grad_send.at[i],
            grads.at[i],
            send_sems.at[2],
            grad_sems.at[i // GROUP],
            ahead(i),
        )

    @pl.loop(0, CHUNKS)
    def _(c):
        line = iota((SLOTS, LANES), 0)
        base = line + c * SLOTS - jnp.where(lax.rem(line, PAD) < CAP, 0, PAD - CAP)
        place = jnp.concatenate(
            [onehot(slot_row[t : t + 1, :].astype(jnp.int32) == base) for t in range(6)], axis=1
        )
        packed = dot(place, grad_pieces[0], 1, 0) + dot(place, grad_pieces[1], 1, 0)
        pack(grad_send, c, packed)

        @pl.when(c == 0)
        def _():
            grads[0] = grad_send[0]

        @pl.loop(0, GROUP)
        def _(g):
            @pl.when(c * GROUP + g > 0)
            def _():
                grad_copy(c * GROUP + g).start()

    @pl.loop(0, CHUNKS)
    def _(c):
        wait_chunk(grads, grad_sems, c)
        high, low = split(unpack(grads, c).T)
        index = index_col[pl.ds(pl.multiple_of(c * SLOTS, SLOTS), SLOTS), :].astype(jnp.int32)
        used = lax.rem(iota((SLOTS, 1), 0), PAD) < CAP
        pick = onehot(jnp.where(used, index, -1) == iota((SLOTS, rows_here), 1))
        summed[...] += dot(high, pick, 1, 0) + dot(low, pick, 1, 0)

    tail = summed[body:width]
    for j in range(1, LANES // TAIL):
        tail = tail + summed[body + TAIL * j : body + TAIL * j + TAIL]
    total = jnp.concatenate([summed[0:body], tail], axis=0)
    new_sum = adagrad[...] + jnp.sum(total * total, axis=0, keepdims=True) * (1.0 / width)
    sum_out[...] = new_sum
    table_out[...] = table[...] - total * (LEARNING_RATE / jnp.sqrt(new_sum))

    part = ask_send.at[pl.ds(1, 7)]
    pltpu.make_async_copy(part, part, send_sems.at[0]).wait()
    part = asked.at[pl.ds(1, 15)]
    pltpu.make_async_copy(part, part, send_sems.at[3]).wait()
    for n, buffer in ((1, row_send), (2, grad_send)):
        part = buffer.at[pl.ds(1, DEVICES - 1)]
        pltpu.make_async_copy(part, part, send_sems.at[n]).wait()
    for dy in range(4):
        forward_copy(dy).wait_send()
        sibling_copy(dy).wait_send()
        if dy > 0:
            home_copy(dy).wait_send()
    for half in range(2):
        half_copy(1, half).wait_send()
        half_copy(3, half).wait_send()
        relay_copy(half).wait_send()


def on_device(entity_table, adagrad_sum, relations, owner_map, head_ids, rel_ids, tail_ids, neg_ids):
    rows_here, width = entity_table.shape
    edges = head_ids.shape[0]
    neg_count = neg_ids.shape[0]
    count = 2 * edges + neg_count
    map_rows = owner_map.shape[0] // 128
    vmem = pl.BlockSpec(memory_space=pltpu.VMEM)
    hbm = pl.BlockSpec(memory_space=pltpu.HBM)
    wide = 4 * LANES
    slots = pltpu.VMEM((DEVICES, LINES, LANES), F32)
    parts = pltpu.VMEM((4, width, LANES), F32)
    sem = pltpu.SemaphoreType.DMA
    new_table, new_sum = pl.pallas_call(
        step_kernel,
        out_shape=(
            jax.ShapeDtypeStruct((width, rows_here), F32),
            jax.ShapeDtypeStruct((1, rows_here), F32),
        ),
        in_specs=[hbm] * 8,
        out_specs=(vmem, vmem),
        scratch_shapes=[
            pltpu.VMEM((1, edges), jnp.int32),
            pltpu.VMEM((1, edges), jnp.int32),
            pltpu.VMEM((neg_count // LANES, LANES), jnp.int32),
            pltpu.VMEM((1, edges), jnp.int32),
            pltpu.VMEM((1, rows_here), F32),
            pltpu.VMEM((map_rows, 128), jnp.int32),
            pltpu.VMEM((width, rows_here), F32),
            pltpu.VMEM((width, -(-relations.shape[0] // (REL * REL_PARTS)) * REL), F32),
            pltpu.VMEM((map_rows, 384), BF16),
            pltpu.VMEM((wide, rows_here), BF16),
            pltpu.VMEM((wide, rows_here), BF16),
            pltpu.VMEM((8, 128), jnp.int32),
            pltpu.VMEM((count, 1), F32),
            pltpu.VMEM((count, 1), F32),
            pltpu.VMEM((count, 1), F32),
            pltpu.VMEM((count, 1), F32),
            pltpu.VMEM((8, 128), F32),
            pltpu.VMEM((8, 16, 1, LANES), F32),
            pltpu.VMEM((8, 16, 1, LANES), F32),
            pltpu.VMEM((16, 1, LANES), F32),
            pltpu.VMEM((16, 1, LANES), F32),
            pltpu.VMEM((DEVICES * PAD, 1), F32),
            slots,
            slots,
            pltpu.VMEM((count, wide), F32),
            pltpu.VMEM((width, edges), F32),
            pltpu.VMEM((edges, wide), F32),
            pltpu.VMEM((2, neg_count, wide), BF16),
            pltpu.VMEM((neg_count, wide), F32),
            pltpu.VMEM((1, neg_count), F32),
            pltpu.VMEM((4, 2, width, LANES), F32),
            pltpu.VMEM((4, 2, width, LANES), F32),
            parts,
            parts,
            parts,
            pltpu.VMEM((2, count, wide), BF16),
            slots,
            slots,
            pltpu.VMEM((wide, rows_here), F32),
            sem((8,)),
            sem((2,)),
            sem((CHUNKS,)),
            sem((CHUNKS,)),
            sem((4, 2)),
            sem((4,)),
            sem((4, 2)),
            sem((4,)),
            sem((4, 2)),
            sem((4,)),
            sem((4, 2)),
        ],
        compiler_params=pltpu.CompilerParams(
            collective_id=0, has_side_effects=True, vmem_limit_bytes=LIMIT
        ),
    )(
        pltpu.with_memory_space_constraint(head_ids.reshape(1, edges), pltpu.HBM),
        pltpu.with_memory_space_constraint(tail_ids.reshape(1, edges), pltpu.HBM),
        pltpu.with_memory_space_constraint(neg_ids.reshape(neg_count // 128, 128), pltpu.HBM),
        pltpu.with_memory_space_constraint(rel_ids.reshape(1, edges), pltpu.HBM),
        pltpu.with_memory_space_constraint(owner_map.reshape(map_rows, 128), pltpu.HBM),
        pltpu.with_memory_space_constraint(entity_table.T, pltpu.HBM),
        pltpu.with_memory_space_constraint(relations.T, pltpu.HBM),
        pltpu.with_memory_space_constraint(adagrad_sum.reshape(1, rows_here), pltpu.HBM),
    )
    return new_table.T, new_sum.reshape(rows_here)


def solution(mesh):
    assert dict(mesh.shape) == {"dp": 16, "blk": 8}
    return jax.shard_map(
        on_device,
        mesh=mesh,
        in_specs=(
            P(("dp", "blk"), None),
            P(("dp", "blk")),
            P(),
            P(),
            P(("dp", "blk")),
            P(("dp", "blk")),
            P(("dp", "blk")),
            P(("dp", "blk")),
        ),
        out_specs=(P(("dp", "blk"), None), P(("dp", "blk"))),
        check_vma=False,
    )
```

```python
import functools

import jax
import jax.numpy as jnp
from jax import lax
from jax.experimental import pallas as pl
from jax.experimental.pallas import tpu as pltpu
from jax.sharding import PartitionSpec as P

MARGIN = 10.0
EPSILON = 1e-05
LEARNING_RATE = 0.1
MESH = pl.DeviceIdType.MESH
F32 = jnp.float32
BF16 = jnp.bfloat16
DEVICES = 128
CAP = 12
PAD = 16
GROUP = 16
CHUNKS = DEVICES // GROUP
SLOTS = GROUP * PAD
LINES = 40
LIMIT = 50 * 1024 * 1024
LANES = 128
TAIL = 16
REL = 256
REL_PARTS = 3


def split(x):
    high = x.astype(BF16)
    return high, (x - high.astype(F32)).astype(BF16)


def dot(a, b, ca, cb):
    return lax.dot_general(a, b, (((ca,), (cb,)), ((), ())), preferred_element_type=F32)


def dot3(a, b, ca, cb):
    return dot(a[0], b[0], ca, cb) + (dot(a[0], b[1], ca, cb) + dot(a[1], b[0], ca, cb))


def iota(shape, axis):
    return lax.broadcasted_iota(jnp.int32, shape, axis)


def onehot(mask):
    return jnp.where(mask, 1.0, 0.0).astype(BF16)


def to_column(row):
    n = row.shape[1]
    return jnp.sum(jnp.where(iota((n, n), 0) == iota((n, n), 1), row, 0.0), axis=1, keepdims=True)


def to_row(column):
    n = column.shape[0]
    return jnp.sum(jnp.where(iota((n, n), 0) == iota((n, n), 1), column, 0.0), axis=0, keepdims=True)


def tail_mask():
    return iota((GROUP, 8, LANES), 1) == iota((GROUP, 8, LANES), 2) // TAIL


def pack(buffer, c, full):
    full = full.reshape(GROUP, PAD, 4 * LANES)
    up, low = full[:, 0:8], full[:, 8:16]
    sub = iota((GROUP, 8, LANES), 1)
    first = sub < 4
    tail_up = jnp.sum(jnp.where(tail_mask(), up[:, :, 3 * LANES :], 0.0), axis=1, keepdims=True)
    tail_low = jnp.sum(
        jnp.where(tail_mask() & first, low[:, :, 3 * LANES :], 0.0), axis=1, keepdims=True
    )
    here = pl.ds(c * GROUP, GROUP)
    for n in range(3):
        buffer[here, 8 * n : 8 * n + 8, :] = up[:, :, LANES * n : LANES * n + LANES]
    buffer[here, 24:32, :] = jnp.where(first, low[:, :, 0:LANES], low[:, :, LANES : 2 * LANES])
    rest = jnp.where(sub == 4, tail_up, jnp.where(sub == 5, tail_low, 0.0))
    buffer[here, 32:40, :] = jnp.where(first, low[:, :, 2 * LANES : 3 * LANES], rest)


def unpack(buffer, c):
    part = buffer[pl.ds(c * GROUP, GROUP)]
    lines = [part[:, 8 * n : 8 * n + 8] for n in range(5)]
    first = iota((GROUP, 8, LANES), 1) < 4
    tail_up = jnp.where(tail_mask(), lines[4][:, 4:5], 0.0)
    tail_low = jnp.where(tail_mask() & first, lines[4][:, 5:6], 0.0)
    turned = pltpu.roll(lines[3].reshape(GROUP * 8, LANES), GROUP * 8 - 4, 0)
    turned = turned.reshape(GROUP, 8, LANES)
    up = jnp.concatenate([lines[0], lines[1], lines[2], tail_up], axis=2)
    low = jnp.concatenate([lines[3], turned, lines[4], tail_low], axis=2)
    return jnp.concatenate([up, low], axis=1).reshape(SLOTS, 4 * LANES)


def to_lines(x):
    tail = x[:, 3 * LANES :]
    for shift in (TAIL, 2 * TAIL, 4 * TAIL):
        tail = tail + pltpu.roll(tail, shift, 1)
    tail = tail.reshape(GROUP, 8, LANES)
    tail = jnp.sum(jnp.where(tail_mask(), tail, 0.0), axis=1)
    return jnp.concatenate([x[:, LANES * n : LANES * n + LANES] for n in range(3)] + [tail], axis=0)


def from_lines(lines):
    tail = lines[3 * LANES :].reshape(GROUP, 1, LANES)
    tail = jnp.where(tail_mask(), tail, 0.0).reshape(LANES, LANES)
    for shift in (4 * TAIL, 2 * TAIL, TAIL):
        tail = tail + pltpu.roll(tail, shift, 1)
    tail = jnp.where(iota((LANES, LANES), 1) < TAIL, tail, 0.0)
    return jnp.concatenate([lines[LANES * n : LANES * n + LANES] for n in range(3)] + [tail], axis=1)


def step_kernel(
    heads_hbm,
    tails_hbm,
    negs_hbm,
    rels_hbm,
    map_hbm,
    table_hbm,
    relations_hbm,
    adagrad_hbm,
    table_out,
    sum_out,
    heads,
    tails,
    negs,
    rels,
    adagrad,
    map_ref,
    table,
    relations,
    map_parts,
    table_high,
    table_low,
    ids,
    key_col,
    ask_col,
    local_col,
    slot_col,
    slot_row,
    ask_send,
    ask_mid,
    ask_sum,
    asked,
    index_col,
    row_send,
    rows,
    wanted,
    rel_acc,
    rel_rows,
    neg_pieces,
    block_acc,
    coef_cols,
    all_queries,
    parts,
    part_sibling,
    part_sum,
    part_recv,
    grad_pieces,
    grad_send,
    grads,
    summed,
    load_sem,
    ask_sems,
    row_sems,
    grad_sems,
    half_sems,
    query_sems,
    part_sems,
    send_sems,
    half_send_sems,
    query_send_sems,
    part_send_sems,
):
    dp = lax.axis_index("dp")
    blk = lax.axis_index("blk")
    mx, mz = dp // 4, lax.rem(dp, 4)
    my, mc = blk // 2, lax.rem(blk, 2)
    width = table.shape[0]
    body = 3 * LANES
    rows_here = table.shape[1]
    edges = heads.shape[1]
    rel_chunks = relations_hbm.shape[1] // REL
    rel_step = relations.shape[1] // REL
    rel_cuts = [min(n * rel_step, rel_chunks) for n in range(REL_PARTS + 1)]

    def deltas(i):
        a, b, c, dc = lax.rem(i, 4), lax.rem(i // 4, 4), lax.rem(i // 16, 4), i // 64
        return a, lax.rem(a + b, 4), lax.rem(a + c, 4), dc

    def ahead(i):
        dx, dy, dz, dc = deltas(i)
        return (
            lax.rem(mx + dx, 4) * 4 + lax.rem(mz + dz, 4),
            lax.rem(my + dy, 4) * 2 + lax.rem(mc + dc, 2),
        )

    def behind(i):
        dx, dy, dz, dc = deltas(i)
        return (
            lax.rem(mx + 4 - dx, 4) * 4 + lax.rem(mz + 4 - dz, 4),
            lax.rem(my + 4 - dy, 4) * 2 + lax.rem(mc + dc, 2),
        )

    def remote(src, dst, send, recv, device):
        return pltpu.make_async_remote_copy(
            src_ref=src,
            dst_ref=dst,
            send_sem=send,
            recv_sem=recv,
            device_id=device,
            device_id_type=MESH,
        )

    barrier = pltpu.get_barrier_semaphore()

    def in_group(r):
        return dp, lax.rem(my + lax.rem(r, 4), 4) * 2 + lax.rem(mc + r // 4, 2)

    def in_plane(p):
        return lax.rem(mx + p // 4, 4) * 4 + lax.rem(mz + lax.rem(p, 4), 4), blk

    @pl.loop(1, 8)
    def _(r):
        pl.semaphore_signal(barrier, inc=1, device_id=in_group(r), device_id_type=MESH)

    @pl.loop(1, 16)
    def _(p):
        pl.semaphore_signal(barrier, inc=1, device_id=in_plane(p), device_id_type=MESH)

    load_map = pltpu.make_async_copy(map_hbm, map_ref, load_sem.at[0])
    load_table = pltpu.make_async_copy(table_hbm, table, load_sem.at[1])

    def load_relations(half):
        first, lanes = rel_cuts[half] * REL, (rel_cuts[half + 1] - rel_cuts[half]) * REL
        part = relations_hbm.at[:, pl.ds(first, lanes)]
        return pltpu.make_async_copy(part, relations.at[:, pl.ds(0, lanes)], load_sem.at[2])

    small = [
        pltpu.make_async_copy(src, dst, load_sem.at[3 + n])
        for n, (src, dst) in enumerate(
            [
                (heads_hbm, heads),
                (tails_hbm, tails),
                (negs_hbm, negs),
                (rels_hbm, rels),
                (adagrad_hbm, adagrad),
            ]
        )
    ]
    for copy in small:
        copy.start()
    load_map.start()
    load_table.start()
    load_relations(0).start()
    for copy in small:
        copy.wait()
    ids[0:1, :] = heads[...]
    ids[1:2, :] = tails[...]
    ids[2:6, :] = negs[...]
    load_map.wait()
    position_of = map_ref[...]
    map_parts[:, 0:128] = (position_of & 255).astype(F32).astype(BF16)
    map_parts[:, 128:256] = ((position_of >> 8) & 255).astype(F32).astype(BF16)
    map_parts[:, 256:384] = (position_of >> 16).astype(F32).astype(BF16)

    @pl.loop(0, 6)
    def _(t):
        column = to_column(ids[pl.ds(t, 1), :].astype(F32)).astype(jnp.int32)
        line = onehot((column >> 7) == iota((128, map_ref.shape[0]), 1))
        found = dot(line, map_parts[...], 1, 0)
        lane = (column & 127) == iota((128, 128), 1)
        piece = [
            jnp.sum(jnp.where(lane, found[:, 128 * p : 128 * p + 128], 0.0), axis=1, keepdims=True)
            for p in range(3)
        ]
        position = (piece[0] + 256.0 * piece[1] + 65536.0 * piece[2]).astype(jnp.int32)
        owner = position >> 11
        dx = ((owner >> 5) - mx) & 3
        dz = ((owner >> 3) - mz) & 3
        dy = ((owner >> 1) - my) & 3
        dc = (owner - mc) & 1
        key = dc * 64 + ((dz - dx) & 3) * 16 + ((dy - dx) & 3) * 4 + dx
        ask = (dc * 4 + dy) * 16 + dx * 4 + dz
        where = pl.ds(pl.multiple_of(t * 128, 128), 128)
        key_col[where, :] = key.astype(F32)
        ask_col[where, :] = ask.astype(F32)
        local_col[where, :] = (position & (rows_here - 1)).astype(F32)

    count = key_col.shape[0]
    keys = key_col[...]
    key_hot = onehot(ask_col[...].astype(jnp.int32) == iota((count, DEVICES), 1))
    earlier = onehot(iota((count, count), 1) < iota((count, count), 0))
    before = dot(earlier, key_hot, 1, 0)
    rank = jnp.sum(before * key_hot.astype(F32), axis=1, keepdims=True)
    local = local_col[...].astype(jnp.int32)
    place = rank.astype(jnp.int32)
    lane = iota((count, LANES), 1)
    spread = lane - (ask_col[...].astype(jnp.int32) // 16) * PAD
    spot = (place == spread) | ((place >= 8) & (place + 4 == spread))
    upper = jnp.where(spot, (local >> 8).astype(F32), 0.0).astype(BF16)
    lower = jnp.where(spot, (local & 255).astype(F32), 0.0).astype(BF16)
    asks = 256.0 * dot(key_hot, upper, 0, 0) + dot(key_hot, lower, 0, 0)
    ask_send[...] = asks.reshape(8, 16, 1, LANES)
    ask_mid[0] = ask_send[0]

    pl.semaphore_wait(barrier, 22)

    def group_ask(r):
        return remote(ask_send.at[r], ask_mid.at[r], send_sems.at[0], ask_sems.at[0], in_group(r))

    def plane_ask(p):
        return remote(ask_sum.at[p], asked.at[p], send_sems.at[3], ask_sems.at[1], in_plane(p))

    @pl.loop(1, 8)
    def _(r):
        group_ask(r).start()

    load_table.wait()
    high, low = split(table[...])
    table_high[0:width] = high
    table_low[0:width] = low
    for j in range(1, LANES // TAIL):
        table_high[body + TAIL * j : body + TAIL * j + TAIL] = high[body:]
        table_low[body + TAIL * j : body + TAIL * j + TAIL] = low[body:]
    summed[...] = jnp.zeros_like(summed)
    wanted[...] = jnp.zeros_like(wanted)
    slot = keys * float(PAD) + rank
    slot_col[...] = slot
    for t in range(6):
        slot_row[t : t + 1, :] = to_row(slot[128 * t : 128 * t + 128])

    part = ask_mid.at[pl.ds(1, 7)]
    pltpu.make_async_copy(part, part, ask_sems.at[0]).wait()
    ask_sum[...] = jnp.sum(ask_mid[...], axis=0)

    @pl.loop(1, 16)
    def _(p):
        plane_ask(p).start()

    asked[0] = ask_sum[0]
    part = asked.at[pl.ds(1, 15)]
    pltpu.make_async_copy(part, part, ask_sems.at[1]).wait()

    def wait_chunk(buffer, sems, c):
        @pl.when(c == 0)
        def _():
            part = buffer.at[pl.ds(1, GROUP - 1)]
            pltpu.make_async_copy(part, part, sems.at[0]).wait()

        @pl.when(c > 0)
        def _():
            part = buffer.at[pl.ds(c * GROUP, GROUP)]
            pltpu.make_async_copy(part, part, sems.at[c]).wait()

    def row_copy(i):
        return remote(
            row_send.at[i],
            rows.at[i],
            send_sems.at[1],
            row_sems.at[i // GROUP],
            behind(i),
        )

    @pl.loop(0, CHUNKS)
    def _(c):
        parts = []
        for g in range(GROUP):
            dx, dy, dz, dc = deltas(c * GROUP + g)
            line = jnp.broadcast_to(asked[dx * 4 + dz], (PAD, LANES))
            lane = iota((PAD, LANES), 1) - (dc * 4 + dy) * PAD
            parts.append(jnp.where(lane == iota((PAD, LANES), 0), line, 0.0))
        index = jnp.sum(jnp.concatenate(parts, axis=0), axis=1, keepdims=True)
        index_col[pl.ds(pl.multiple_of(c * SLOTS, SLOTS), SLOTS), :] = index
        pick = onehot(index.astype(jnp.int32) == iota((SLOTS, rows_here), 1))
        picked = dot(pick, table_high[...], 1, 1) + dot(pick, table_low[...], 1, 1)
        pack(row_send, c, picked)

        @pl.when(c == 0)
        def _():
            rows[0] = row_send[0]

        @pl.loop(0, GROUP)
        def _(g):
            @pl.when(c * GROUP + g > 0)
            def _():
                row_copy(c * GROUP + g).start()

    rel_acc[...] = jnp.zeros_like(rel_acc)
    for half in range(REL_PARTS):
        load_relations(half).wait()

        @pl.loop(0, rel_cuts[half + 1] - rel_cuts[half])
        def _(t):
            high, low = split(relations[:, pl.ds(pl.multiple_of(t * REL, REL), REL)])
            base = (t + rel_cuts[half]) * REL
            pick = onehot(iota((REL, edges), 0) + base == rels[...])
            found = dot(jnp.concatenate([high, low], axis=0), pick, 1, 0)
            rel_acc[...] += found[0:width] + found[width:]

        if half + 1 < REL_PARTS:
            load_relations(half + 1).start()

    rel_rows[...] = jnp.zeros_like(rel_rows)
    rel_rows[:, 0:width] = rel_acc[...].T

    @pl.loop(0, CHUNKS)
    def _(c):
        wait_chunk(rows, row_sems, c)
        high, low = split(unpack(rows, c))
        place = onehot(slot_col[...].astype(jnp.int32) - c * SLOTS == iota((count, SLOTS), 1))
        wanted[...] += dot(place, high, 1, 0) + dot(place, low, 1, 0)

    high, low = split(wanted[:, body:])
    fold = onehot(lax.rem(iota((LANES, LANES), 0), TAIL) == iota((LANES, LANES), 1))
    wanted[:, body:] = dot(high, fold, 1, 0) + dot(low, fold, 1, 0)
    queries = wanted[0:edges, :] + rel_rows[...]
    residue = queries - wanted[edges : 2 * edges, :]
    pos_dist = jnp.sqrt(jnp.sum(residue * residue, axis=1, keepdims=True) + EPSILON)
    grad_pos = (1.0 / (1.0 + jnp.exp(MARGIN - pos_dist)) / pos_dist) * residue
    all_queries[0, 0] = to_lines(queries)

    sibling = (dp, blk + 1 - 2 * mc)

    def at_y(dy):
        return dp, lax.rem(my + dy, 4) * 2 + mc

    def half_copy(dy, half):
        lines = pl.ds(half * (width // 2), width // 2)
        return remote(
            all_queries.at[0, 0, lines, :],
            all_queries.at[dy, 0, lines, :],
            half_send_sems.at[dy, half],
            half_sems.at[dy, half],
            at_y(dy),
        )

    def relay_copy(half):
        lines = pl.ds(half * (width // 2), width // 2)
        return remote(
            all_queries.at[1 + 2 * half, 0, lines, :],
            all_queries.at[2, 0, lines, :],
            half_send_sems.at[2, half],
            half_sems.at[2, half],
            at_y(1 + 2 * half),
        )

    def forward_copy(dy):
        return remote(
            all_queries.at[dy, 0],
            all_queries.at[dy, 1],
            query_send_sems.at[dy],
            query_sems.at[dy],
            sibling,
        )

    for dy, half in ((1, 0), (3, 1), (1, 1), (3, 0)):
        half_copy(dy, half).start()
    forward_copy(0).start()
    negatives = wanted[2 * edges :, :]
    high, low = split(negatives)
    neg_pieces[0] = high
    neg_pieces[1] = low
    neg_col = jnp.sum(negatives * negatives, axis=1, keepdims=True)
    neg_count = negatives.shape[0]
    neg_sq = jnp.concatenate(
        [to_row(neg_col[128 * t : 128 * t + 128]) for t in range(neg_count // 128)], axis=1
    )
    block_acc[...] = jnp.zeros_like(block_acc)
    coef_cols[...] = jnp.zeros_like(coef_cols)
    weight = 8.0 * neg_count

    def sibling_copy(dy):
        return remote(
            parts.at[dy, 1],
            part_sibling.at[dy],
            part_send_sems.at[dy, 0],
            part_sems.at[dy, 0],
            sibling,
        )

    def home_copy(dy):
        return remote(
            part_sum.at[dy],
            part_recv.at[dy],
            part_send_sems.at[dy, 1],
            part_sems.at[dy, 1],
            (dp, lax.rem(my + 4 - dy, 4) * 2 + mc),
        )

    def block_terms(block, where):
        pieces = split(block)
        block_sq = jnp.sum(block * block, axis=1, keepdims=True)
        neg_parts = (neg_pieces[0], neg_pieces[1])
        both = dot(jnp.concatenate(pieces, axis=0), neg_parts[0], 1, 1)
        inner = both[0:edges] + (both[edges:] + dot(pieces[0], neg_parts[1], 1, 1))
        dist = jnp.sqrt(block_sq + neg_sq - 2.0 * inner + EPSILON)
        coef = -1.0 / ((1.0 + jnp.exp(dist - MARGIN)) * (weight * dist))
        coef_parts = split(coef)
        coef_cols[...] += jnp.sum(coef, axis=0, keepdims=True)
        block_acc[...] += dot3(coef_parts, pieces, 0, 0)
        both = dot(jnp.concatenate(coef_parts, axis=0), neg_parts[0], 1, 0)
        drawn = both[0:edges] + (both[edges:] + dot(coef_parts[0], neg_parts[1], 1, 0))
        return block * jnp.sum(coef, axis=1, keepdims=True) - drawn

    def finish(dy):
        sibling_copy(dy).wait_recv()
        part_sum[dy] = parts[dy, 0] + part_sibling[dy]

    @pl.loop(0, 8)
    def _(u):
        v, w = u // 2, lax.rem(u, 2)
        far = (v + 1) // 2
        dy = far + lax.rem(far, 2) * 2 * w
        dc = v // 2 + (1 - (lax.rem(v, 3) + 1) // 2) * w * (1 - 2 * (v // 2))

        @pl.when(u == 2)
        def _():
            half_copy(1, 0).wait_recv()
            relay_copy(0).start()
            half_copy(3, 1).wait_recv()
            relay_copy(1).start()
            half_copy(1, 1).wait_recv()
            forward_copy(1).start()
            half_copy(3, 0).wait_recv()
            forward_copy(3).start()

        @pl.when(u == 4)
        def _():
            relay_copy(0).wait_recv()
            relay_copy(1).wait_recv()
            forward_copy(2).start()

        @pl.when(dc == 1)
        def _():
            forward_copy(dy).wait_recv()

        where = pl.ds(pl.multiple_of(u * edges, edges), edges)
        parts[dy, dc] = to_lines(block_terms(from_lines(all_queries[dy, dc]), where))

        @pl.when(dc == 1)
        def _():
            sibling_copy(dy).start()

        @pl.when((u == 5) | (u == 6))
        def _():
            last = 1 + 2 * (u - 5)
            finish(last)
            home_copy(last).start()

    finish(2)
    home_copy(2).start()
    finish(0)
    coef_col = jnp.concatenate(
        [to_column(coef_cols[:, 128 * t : 128 * t + 128]) for t in range(neg_count // 128)], axis=0
    )
    spread = onehot(iota((LANES, LANES), 0) == lax.rem(iota((LANES, LANES), 1), TAIL))

    def keep(first, last, value):
        for n, piece in enumerate(split(value)):
            grad_pieces[n, first:last, 0:body] = piece[:, 0:body]
            grad_pieces[n, first:last, body:] = dot(piece[:, body:], spread, 1, 0).astype(BF16)

    keep(edges, 2 * edges, -grad_pos)
    keep(2 * edges, count, wanted[2 * edges :, :] * coef_col - block_acc[...])
    for dy in (1, 3, 2):
        home_copy(dy).wait_recv()
    grad_neg = from_lines((part_sum[0] + part_recv[1]) + (part_recv[2] + part_recv[3]))
    keep(0, edges, grad_pos + grad_neg)

    def grad_copy(i):
        return remote(
            grad_send.at[i],
            grads.at[i],
            send_sems.at[2],
            grad_sems.at[i // GROUP],
            ahead(i),
        )

    @pl.loop(0, CHUNKS)
    def _(c):
        line = iota((SLOTS, LANES), 0)
        base = line + c * SLOTS - jnp.where(lax.rem(line, PAD) < CAP, 0, PAD - CAP)
        place = jnp.concatenate(
            [onehot(slot_row[t : t + 1, :].astype(jnp.int32) == base) for t in range(6)], axis=1
        )
        packed = dot(place, grad_pieces[0], 1, 0) + dot(place, grad_pieces[1], 1, 0)
        pack(grad_send, c, packed)

        @pl.when(c == 0)
        def _():
            grads[0] = grad_send[0]

        @pl.loop(0, GROUP)
        def _(g):
            @pl.when(c * GROUP + g > 0)
            def _():
                grad_copy(c * GROUP + g).start()

    @pl.loop(0, CHUNKS)
    def _(c):
        wait_chunk(grads, grad_sems, c)
        high, low = split(unpack(grads, c).T)
        index = index_col[pl.ds(pl.multiple_of(c * SLOTS, SLOTS), SLOTS), :].astype(jnp.int32)
        used = lax.rem(iota((SLOTS, 1), 0), PAD) < CAP
        pick = onehot(jnp.where(used, index, -1) == iota((SLOTS, rows_here), 1))
        summed[...] += dot(high, pick, 1, 0) + dot(low, pick, 1, 0)

    tail = summed[body:width]
    for j in range(1, LANES // TAIL):
        tail = tail + summed[body + TAIL * j : body + TAIL * j + TAIL]
    total = jnp.concatenate([summed[0:body], tail], axis=0)
    new_sum = adagrad[...] + jnp.sum(total * total, axis=0, keepdims=True) * (1.0 / width)
    sum_out[...] = new_sum
    table_out[...] = table[...] - total * (LEARNING_RATE / jnp.sqrt(new_sum))

    part = ask_send.at[pl.ds(1, 7)]
    pltpu.make_async_copy(part, part, send_sems.at[0]).wait()
    part = asked.at[pl.ds(1, 15)]
    pltpu.make_async_copy(part, part, send_sems.at[3]).wait()
    for n, buffer in ((1, row_send), (2, grad_send)):
        part = buffer.at[pl.ds(1, DEVICES - 1)]
        pltpu.make_async_copy(part, part, send_sems.at[n]).wait()
    for dy in range(4):
        forward_copy(dy).wait_send()
        sibling_copy(dy).wait_send()
        if dy > 0:
            home_copy(dy).wait_send()
    for half in range(2):
        half_copy(1, half).wait_send()
        half_copy(3, half).wait_send()
        relay_copy(half).wait_send()


def on_device(entity_table, adagrad_sum, relations, owner_map, head_ids, rel_ids, tail_ids, neg_ids):
    rows_here, width = entity_table.shape
    edges = head_ids.shape[0]
    neg_count = neg_ids.shape[0]
    count = 2 * edges + neg_count
    map_rows = owner_map.shape[0] // 128
    vmem = pl.BlockSpec(memory_space=pltpu.VMEM)
    hbm = pl.BlockSpec(memory_space=pltpu.HBM)
    wide = 4 * LANES
    slots = pltpu.VMEM((DEVICES, LINES, LANES), F32)
    parts = pltpu.VMEM((4, width, LANES), F32)
    sem = pltpu.SemaphoreType.DMA
    new_table, new_sum = pl.pallas_call(
        step_kernel,
        out_shape=(
            jax.ShapeDtypeStruct((width, rows_here), F32),
            jax.ShapeDtypeStruct((1, rows_here), F32),
        ),
        in_specs=[hbm] * 8,
        out_specs=(vmem, vmem),
        scratch_shapes=[
            pltpu.VMEM((1, edges), jnp.int32),
            pltpu.VMEM((1, edges), jnp.int32),
            pltpu.VMEM((neg_count // LANES, LANES), jnp.int32),
            pltpu.VMEM((1, edges), jnp.int32),
            pltpu.VMEM((1, rows_here), F32),
            pltpu.VMEM((map_rows, 128), jnp.int32),
            pltpu.VMEM((width, rows_here), F32),
            pltpu.VMEM((width, -(-relations.shape[0] // (REL * REL_PARTS)) * REL), F32),
            pltpu.VMEM((map_rows, 384), BF16),
            pltpu.VMEM((wide, rows_here), BF16),
            pltpu.VMEM((wide, rows_here), BF16),
            pltpu.VMEM((8, 128), jnp.int32),
            pltpu.VMEM((count, 1), F32),
            pltpu.VMEM((count, 1), F32),
            pltpu.VMEM((count, 1), F32),
            pltpu.VMEM((count, 1), F32),
            pltpu.VMEM((8, 128), F32),
            pltpu.VMEM((8, 16, 1, LANES), F32),
            pltpu.VMEM((8, 16, 1, LANES), F32),
            pltpu.VMEM((16, 1, LANES), F32),
            pltpu.VMEM((16, 1, LANES), F32),
            pltpu.VMEM((DEVICES * PAD, 1), F32),
            slots,
            slots,
            pltpu.VMEM((count, wide), F32),
            pltpu.VMEM((width, edges), F32),
            pltpu.VMEM((edges, wide), F32),
            pltpu.VMEM((2, neg_count, wide), BF16),
            pltpu.VMEM((neg_count, wide), F32),
            pltpu.VMEM((1, neg_count), F32),
            pltpu.VMEM((4, 2, width, LANES), F32),
            pltpu.VMEM((4, 2, width, LANES), F32),
            parts,
            parts,
            parts,
            pltpu.VMEM((2, count, wide), BF16),
            slots,
            slots,
            pltpu.VMEM((wide, rows_here), F32),
            sem((8,)),
            sem((2,)),
            sem((CHUNKS,)),
            sem((CHUNKS,)),
            sem((4, 2)),
            sem((4,)),
            sem((4, 2)),
            sem((4,)),
            sem((4, 2)),
            sem((4,)),
            sem((4, 2)),
        ],
        compiler_params=pltpu.CompilerParams(
            collective_id=0, has_side_effects=True, vmem_limit_bytes=LIMIT
        ),
    )(
        pltpu.with_memory_space_constraint(head_ids.reshape(1, edges), pltpu.HBM),
        pltpu.with_memory_space_constraint(tail_ids.reshape(1, edges), pltpu.HBM),
        pltpu.with_memory_space_constraint(neg_ids.reshape(neg_count // 128, 128), pltpu.HBM),
        pltpu.with_memory_space_constraint(rel_ids.reshape(1, edges), pltpu.HBM),
        pltpu.with_memory_space_constraint(owner_map.reshape(map_rows, 128), pltpu.HBM),
        pltpu.with_memory_space_constraint(entity_table.T, pltpu.HBM),
        pltpu.with_memory_space_constraint(relations.T, pltpu.HBM),
        pltpu.with_memory_space_constraint(adagrad_sum.reshape(1, rows_here), pltpu.HBM),
    )
    return new_table.T, new_sum.reshape(rows_here)


def solution(mesh):
    assert dict(mesh.shape) == {"dp": 16, "blk": 8}
    return jax.shard_map(
        on_device,
        mesh=mesh,
        in_specs=(
            P(("dp", "blk"), None),
            P(("dp", "blk")),
            P(),
            P(),
            P(("dp", "blk")),
            P(("dp", "blk")),
            P(("dp", "blk")),
            P(("dp", "blk")),
        ),
        out_specs=(P(("dp", "blk"), None), P(("dp", "blk"))),
        check_vma=False,
    )
```
